512 devices in a mesh: dp: 32 (over z, core), seq: 16 (over y, x).
Axes of the slice: x: 4, y: 4, z: 16, core: 2. Of those that a mesh axis runs over, the one named last changes fastest.
Arguments:
- features: bfloat16 [32, 3072, 1024], P('dp', 'seq'), may hold values from -18 to 18
- qkv_weight: bfloat16 [1024, 3072], P('dp'), may hold values from -1 to 1
- cotangent: bfloat16 [32, 3072, 1024], P('dp', 'seq'), may hold values from -6 to 6
- node_order: int32 [32, 3072], P('dp'), may hold values from 0 to 3071, as said below
- blocks: int32 [32, 48, 8], P('dp'), may hold values from 0 to 47, as said below
- counts: int32 [32, 48], P('dp'), may hold values from 1 to 8, as said below
Outputs:
- attended: bfloat16 [32, 3072, 1024], P('dp', 'seq')
- grad_features: bfloat16 [32, 3072, 1024], P('dp', 'seq')
- grad_weight: float32 [1024, 3072], P('dp', 'seq')
The draws below stay inside these ranges and needn't reach their ends.
Inputs may be any that keep to these rules, and one draw needn't show every extreme that they name: Every row of node_order lists each node of the subgraph once. blocks[g, c, 0] is c, and the 8 entries of a row are distinct clusters; slots at or beyond counts[g, c] are unused. `counts`: every subgraph has a cluster with all 8 slots live.
All inputs are finite; a program needn't handle non-finite values.
Results may differ from the reference program's by a relative error of at most 0.03.
Values may be sent and summed in bfloat16 or wider, within the bound.
No kernel may reach another device: no remote copies, remote signals or barrier semaphores. Data moves between devices by JAX's collectives and lax.ppermute only.
A program may use at most 128 MiB of HBM per device.

```python
import math
import jax
import jax.numpy as jnp
from jax import lax

HEADS = 16
HD = 64
D = 1024
MAXB = 8
GRAPHS = 32
NODES = 3072
CLUSTERS = 48


def draw_blocks(key, part):
    row_keys = jax.random.split(key, GRAPHS * CLUSTERS)
    others_list = jnp.arange(1, CLUSTERS, dtype=jnp.int32)

    def pick_offsets(one_key):
        return jax.random.permutation(one_key, others_list)[:MAXB - 1]
    offsets = jax.vmap(pick_offsets)(row_keys)
    offsets = jnp.concatenate([jnp.zeros((GRAPHS * CLUSTERS, 1), jnp.int32), offsets], axis=1)
    own_ids = jnp.tile(jnp.arange(CLUSTERS, dtype=jnp.int32), GRAPHS)
    result = (own_ids[:, None] + offsets) % CLUSTERS
    return result.reshape(GRAPHS, CLUSTERS, MAXB).astype(jnp.int32)


def draw_counts(key, part):
    first_key, second_key = jax.random.split(key)
    values = jax.random.randint(first_key, (GRAPHS, CLUSTERS), 1, MAXB + 1)
    full_at = jax.random.randint(second_key, (GRAPHS,), 0, CLUSTERS)
    marked = jnp.arange(CLUSTERS)[None, :] == full_at[:, None]
    return jnp.where(marked, MAXB, values).astype(jnp.int32)


def orders_all(key):
    graph_keys = jax.random.split(jax.random.fold_in(key, 11), GRAPHS)
    node_ids = jnp.arange(NODES, dtype=jnp.int32)

    def one_order(one_key):
        return jax.random.permutation(one_key, node_ids)
    return jax.vmap(one_order)(graph_keys).astype(jnp.int32)


def draw_node_order(key, part):
    return orders_all(key)


def draw_features(key, part):
    base_key, pair_key = jax.random.split(jax.random.fold_in(key, 23), 2)
    column_ids = jnp.arange(D)[None, None, :]
    fresh_values = jnp.clip(jax.random.normal(base_key, (GRAPHS, NODES, D), jnp.float32), -6.0, 6.0)
    pairing = jax.random.permutation(pair_key, GRAPHS)
    spiked = column_ids // (D // GRAPHS) == pairing[:, None, None]
    fresh_values = jnp.where(spiked, 3.0 * fresh_values, fresh_values)
    return fresh_values.astype(jnp.bfloat16)


def draw_qkv_weight(key, part):
    first_key = jax.random.fold_in(key, 31)
    fresh_values = jnp.clip(jax.random.normal(first_key, (D, 3 * D), jnp.float32), -6.0, 6.0)
    return (fresh_values * D ** (-0.5)).astype(jnp.bfloat16)


def level_of(own_key, extent, pieces, smallest, largest):
    loudness = 1.0
    for position, blocks in pieces:
        heights = jax.random.uniform(jax.random.fold_in(jax.random.fold_in(own_key, 6), position), (blocks,), jnp.float32, smallest / len(pieces), largest / len(pieces))
        loudness = loudness * jnp.repeat(jnp.exp(heights), extent[position] // blocks).reshape((-1,) + (1,) * (len(extent) - 1 - position))
    return loudness


def noise(key, dims, scale, reach, cuts=(), kind=jnp.bfloat16):
    factor_of = level_of(key, dims, cuts, -0.22, 0.18) if cuts else 1.0
    drawn = jax.random.normal(key, dims, jnp.float32) * scale * factor_of
    return jnp.minimum(jnp.maximum(drawn, -reach), reach).astype(kind)


def setup_inputs(seed: int = 0) -> dict:
    keys = jax.random.split(jax.random.key(seed), 7)
    return {
        "features": draw_features(jax.random.fold_in(keys[6], 71), 0),
        "qkv_weight": draw_qkv_weight(jax.random.fold_in(keys[6], 71), 0),
        "cotangent": noise(keys[2], (GRAPHS, NODES, D), 1.0, 6.0, ((0, 32), (1, 16))),
        "node_order": draw_node_order(jax.random.fold_in(keys[6], 71), 0),
        "blocks": draw_blocks(jax.random.fold_in(keys[6], 71), 0),
        "counts": draw_counts(jax.random.fold_in(keys[6], 71), 0),
    }


def attend(query, key_in, value, grad_out, blocks, counts):
    cluster_count, slot_count = blocks.shape
    node_count, head_width = query.shape
    block_rows = node_count // cluster_count
    score_scale = 1.0 / math.sqrt(head_width)
    key_blocks = key_in.reshape(cluster_count, block_rows, head_width).astype(jnp.float32)
    value_blocks = value.reshape(cluster_count, block_rows, head_width).astype(jnp.float32)
    query_block = query.reshape(cluster_count, block_rows, head_width).astype(jnp.float32)
    grad_block = grad_out.reshape(cluster_count, block_rows, head_width).astype(jnp.float32)
    key_rows = key_blocks[blocks].reshape(cluster_count, slot_count * block_rows, head_width)
    value_rows = value_blocks[blocks].reshape(cluster_count, slot_count * block_rows, head_width)
    is_live = jnp.repeat(jnp.arange(slot_count)[None, :] < counts[:, None], block_rows, axis=1)[:, None, :]
    scores = jnp.einsum('cqe,cke->cqk', query_block, key_rows) * score_scale
    scores = jnp.where(is_live, scores, -1e+30)
    row_max = lax.optimization_barrier(jnp.max(scores, axis=-1, keepdims=True))
    raw_weights = jnp.where(is_live, jnp.exp(scores - row_max), 0.0)
    attn_weights = raw_weights / lax.optimization_barrier(jnp.sum(raw_weights, axis=-1, keepdims=True))
    attn_low = lax.optimization_barrier(attn_weights.astype(jnp.bfloat16)).astype(jnp.float32)
    output_all = jnp.einsum('cqk,cke->cqe', attn_low, value_rows).astype(jnp.bfloat16)
    grad_weights = jnp.einsum('cqe,cke->cqk', grad_block, value_rows)
    row_dot = lax.optimization_barrier(jnp.sum(attn_weights * grad_weights, axis=-1, keepdims=True))
    grad_scores = attn_weights * (grad_weights - row_dot) * score_scale
    grad_scores = lax.optimization_barrier(grad_scores.astype(jnp.bfloat16)).astype(jnp.float32)
    grad_query = jnp.einsum('cqk,cke->cqe', grad_scores, key_rows).astype(jnp.bfloat16)
    key_terms = jnp.einsum('cqk,cqe->cke', grad_scores, query_block).reshape(cluster_count, slot_count, block_rows, head_width)
    value_terms = jnp.einsum('cqk,cqe->cke', attn_low, grad_block).reshape(cluster_count, slot_count, block_rows, head_width)
    empty_sum = jnp.zeros((cluster_count, block_rows, head_width), jnp.float32)
    grad_key = empty_sum.at[blocks].add(key_terms)
    grad_value = empty_sum.at[blocks].add(value_terms)
    return (output_all.reshape(node_count, head_width), grad_query.reshape(node_count, head_width), grad_key.reshape(node_count, head_width).astype(jnp.bfloat16), grad_value.reshape(node_count, head_width).astype(jnp.bfloat16))

def reference(features, qkv_weight, cotangent, node_order, blocks, counts):
    graphs, node_count, model_width = features.shape

    def per_graph(totals, inputs_now):
        graph_feats, graph_cot, graph_order, block_ids, live_count = inputs_now
        projected = jnp.dot(graph_feats, qkv_weight, preferred_element_type=jnp.float32).astype(jnp.bfloat16)
        projected = projected.reshape(node_count, HEADS, 3 * HD)
        inverse = jnp.zeros((node_count,), jnp.int32).at[graph_order].set(jnp.arange(node_count, dtype=jnp.int32))
        sorted_qkv = projected[graph_order]
        sorted_cot = graph_cot.reshape(node_count, HEADS, HD)[graph_order]
        output_all, grad_query, grad_key, grad_value = jax.vmap(attend, in_axes=(1, 1, 1, 1, None, None), out_axes=1)(sorted_qkv[:, :, :HD], sorted_qkv[:, :, HD:2 * HD], sorted_qkv[:, :, 2 * HD:], sorted_cot, block_ids, live_count)
        grad_all = jnp.concatenate([grad_query, grad_key, grad_value], axis=-1)[inverse].reshape(node_count, 3 * model_width)
        output_nodes = output_all[inverse].reshape(node_count, model_width)
        grad_feats = jnp.dot(grad_all, qkv_weight.T, preferred_element_type=jnp.float32).astype(jnp.bfloat16)
        totals = totals + jnp.dot(graph_feats.T, grad_all, preferred_element_type=jnp.float32)
        return (totals, (output_nodes, grad_feats))
    start_sum = jnp.zeros((model_width, 3 * model_width), jnp.float32)
    grad_weight, (attended, grad_features) = lax.scan(per_graph, start_sum, (features, cotangent, node_order, blocks, counts))
    return (attended, grad_features, grad_weight)
```

```python
import jax
import jax.numpy as jnp
from jax import lax
from jax.experimental import pallas as pl
from jax.experimental.pallas import tpu as pltpu
from jax.sharding import PartitionSpec as P

HEADS = 16
HD = 64
BF = jnp.bfloat16
F32 = jnp.float32
ROWS = 256


def dot(a, b, ca=1, cb=0):
    return lax.dot_general(a, b, (((ca,), (cb,)), ((), ())), preferred_element_type=F32)


def attend_kernel(
    blocks_ref, counts_ref, feat_ref, w_ref, cot_ref, ocol_ref, orow_ref,
    out_ref, x_ref, kv_ref, a_ref, acc_ref, g_ref,
):
    nodes = feat_ref.shape[0]
    clusters, slots = blocks_ref.shape
    rows = nodes // clusters
    keys = slots * rows
    tiles = nodes // ROWS
    place = (
        lax.broadcasted_iota(jnp.int32, (HD, 4 * HD), 0) + 3 * HD
        == lax.broadcasted_iota(jnp.int32, (HD, 4 * HD), 1)
    ).astype(F32).astype(BF)

    def project(i, carry):
        r = pl.ds(pl.multiple_of(i * ROWS, ROWS), ROWS)
        x = dot(feat_ref[r, :], w_ref[...]) + dot(cot_ref[r, :], place)
        x_ref[r, :] = x.astype(BF)
        return carry

    lax.fori_loop(0, tiles, project, 0, unroll=2)

    first = lax.broadcasted_iota(jnp.int32, (rows, 2 * HD), 1) < HD

    def to_clusters(i, carry):
        r = pl.ds(pl.multiple_of(i * ROWS, ROWS), ROWS)
        pick = ocol_ref[r, :] == lax.broadcasted_iota(jnp.int32, (ROWS, nodes), 1)
        moved = dot(pick.astype(F32).astype(BF), x_ref[...])
        kv_ref[r, :] = moved[:, : 2 * HD].astype(BF)
        for t in range(ROWS // rows):
            qd = moved[t * rows : (t + 1) * rows, 2 * HD :]
            base = pl.multiple_of(i * 2 * ROWS + 2 * rows * t, 2 * rows)
            a_ref[pl.ds(base, rows), :] = jnp.where(first, qd, 0.0).astype(BF)
            a_ref[pl.ds(base + rows, rows), :] = jnp.where(first, 0.0, qd).astype(BF)
        return carry

    lax.fori_loop(0, tiles, to_clusters, 0, unroll=1)

    acc_ref[...] = jnp.zeros_like(acc_ref)
    key_at = lax.broadcasted_iota(jnp.int32, (rows, keys), 1)

    def cluster(c):
        at = [
            pl.ds(pl.multiple_of(blocks_ref[c, j] * rows, rows), rows)
            for j in range(slots)
        ]
        kv = jnp.concatenate([kv_ref[s, :] for s in at], axis=0)
        a = a_ref[pl.ds(pl.multiple_of(c * 2 * rows, 2 * rows), 2 * rows), :]
        both = dot(a, kv, 1, 1)
        score = jnp.where(key_at < counts_ref[c] * rows, both[:rows], -1e30)
        dpw = both[rows:]
        raw = jnp.exp(score - jnp.max(score, axis=1, keepdims=True))
        p = raw * (1.0 / jnp.sum(raw, axis=1, keepdims=True))
        ds = p * (dpw - jnp.sum(p * dpw, axis=1, keepdims=True))
        pd = jnp.concatenate([ds, p], axis=0).astype(BF)
        oq = dot(pd, kv)
        back = dot(pd, a, 0, 0)
        here = pl.ds(pl.multiple_of(c * rows, rows), rows)
        g_ref[here, 2 * HD :] = jnp.where(first, oq[:rows] * 0.125, oq[rows:]).astype(BF)
        return at, back

    def step(i, carry):
        for c in (2 * i, 2 * i + 1):
            at, back = cluster(c)
            new = [
                acc_ref[s, :] + back[j * rows : (j + 1) * rows]
                for j, s in enumerate(at)
            ]
            for s, v in zip(at, new):
                acc_ref[s, :] = v
        return carry

    lax.fori_loop(0, clusters // 2, step, 0)
    g_ref[:, : 2 * HD] = acc_ref[...].astype(BF)

    def to_nodes(i, carry):
        r = pl.ds(pl.multiple_of(i * ROWS, ROWS), ROWS)
        pick = orow_ref[...] == lax.broadcasted_iota(jnp.int32, (ROWS, nodes), 0) + i * ROWS
        out_ref[r, :] = dot(pick.astype(F32).astype(BF), g_ref[...]).astype(BF)
        return carry

    lax.fori_loop(0, tiles, to_nodes, 0, unroll=1)


def attend(feats, w_head, cot, order, blocks, counts):
    nodes = feats.shape[0]
    vmem = pl.BlockSpec(memory_space=pltpu.VMEM)
    smem = pl.BlockSpec(memory_space=pltpu.SMEM)
    return pl.pallas_call(
        attend_kernel,
        name="attend",
        out_shape=jax.ShapeDtypeStruct((nodes, 4 * HD), BF),
        in_specs=[smem, smem] + [vmem] * 5,
        out_specs=vmem,
        scratch_shapes=[
            pltpu.VMEM((nodes, 4 * HD), BF),
            pltpu.VMEM((nodes, 2 * HD), BF),
            pltpu.VMEM((2 * nodes, 2 * HD), BF),
            pltpu.VMEM((nodes, 2 * HD), F32),
            pltpu.VMEM((nodes, 4 * HD), BF),
        ],
        compiler_params=pltpu.CompilerParams(vmem_limit_bytes=50 << 20),
    )(blocks, counts, feats, w_head, cot, order.reshape(nodes, 1), order.reshape(1, nodes))


def finish_kernel(g_ref, w_ref, att_ref, gf_ref, lhs_ref):
    heads = g_ref.shape[0]
    wide = heads * 2 * HD
    first = lax.broadcasted_iota(jnp.int32, (g_ref.shape[1], 2 * HD), 1) < HD
    for h in range(0, heads, 2):
        lhs_ref[:, h * 2 * HD : (h + 1) * 2 * HD] = g_ref[h, :, : 2 * HD]
        lhs_ref[:, (h + 1) * 2 * HD : (h + 2) * 2 * HD] = g_ref[h + 1, :, : 2 * HD]
        even = g_ref[h, :, 2 * HD :].astype(F32)
        odd = g_ref[h + 1, :, 2 * HD :].astype(F32)
        to = slice(h * HD, (h + 2) * HD)
        lhs_ref[:, wide + h * HD : wide + (h + 2) * HD] = jnp.where(
            first, even, pltpu.roll(odd, HD, 1)
        ).astype(BF)
        att_ref[:, to] = jnp.where(first, pltpu.roll(even, HD, 1), odd).astype(BF)
    gf_ref[...] = dot(lhs_ref[...], w_ref[...], 1, 1).astype(BF)


def finish(got, weights):
    rows, width = got.shape[1], weights.shape[0]
    vmem = pl.BlockSpec(memory_space=pltpu.VMEM)
    return pl.pallas_call(
        finish_kernel,
        name="finish",
        out_shape=[
            jax.ShapeDtypeStruct((rows, HEADS * HD), BF),
            jax.ShapeDtypeStruct((rows, width), BF),
        ],
        in_specs=[vmem, vmem],
        out_specs=[vmem, vmem],
        scratch_shapes=[pltpu.VMEM((rows, weights.shape[1]), BF)],
        compiler_params=pltpu.CompilerParams(vmem_limit_bytes=40 << 20),
    )(got, weights)


def per_device(features, qkv_weight, cotangent, node_order, blocks, counts):
    local_rows = features.shape[1]
    model_width = features.shape[2]
    deep = qkv_weight.shape[0]
    feats = features[0]
    head = lax.axis_index("seq")
    own = lax.dynamic_slice(qkv_weight, (0, head * 3 * HD), (deep, 3 * HD))
    own = jnp.concatenate(
        [own[:, HD:], own[:, :HD] * jnp.asarray(0.125, BF), jnp.zeros((deep, HD), BF)],
        axis=1,
    )
    w_head = lax.all_gather(own, "dp", axis=0, tiled=True)
    node_all = lax.all_gather(feats, "seq", axis=0, tiled=True)
    cot = lax.all_to_all(
        cotangent[0].reshape(local_rows, HEADS, HD).transpose(1, 0, 2), "seq", 0, 0, tiled=True
    ).reshape(HEADS * local_rows, HD)
    by_head = qkv_weight.reshape(deep, HEADS, 3 * HD)
    ordered = jnp.concatenate(
        [by_head[:, :, HD:].reshape(deep, -1), by_head[:, :, :HD].reshape(deep, -1)], axis=1
    )
    weights = lax.all_gather(ordered, "dp", axis=0, tiled=True)
    grads = attend(node_all, w_head, cot, node_order[0], blocks[0], counts[0])
    got = lax.all_to_all(grads.reshape(HEADS, local_rows, 4 * HD), "seq", 0, 0, tiled=True)
    part = lax.dot_general(
        node_all, grads[:, : 3 * HD], (((0,), (0,)), ((), ())), preferred_element_type=F32
    ).astype(BF)
    parts = lax.all_to_all(part.reshape(-1, deep, 3 * HD), "dp", 0, 0, tiled=True)
    total = jnp.sum(parts.astype(F32), axis=0)
    grad_weight = jnp.concatenate([total[:, 2 * HD :], total[:, : 2 * HD]], axis=1)
    attended, grad_feats = finish(got, weights)
    return (
        attended.reshape(1, local_rows, model_width),
        grad_feats.reshape(1, local_rows, model_width),
        grad_weight,
    )


def solution(mesh):
    return jax.shard_map(
        per_device,
        mesh=mesh,
        in_specs=(
            P("dp", "seq", None),
            P("dp", None),
            P("dp", "seq", None),
            P("dp", None),
            P("dp", None, None),
            P("dp", None),
        ),
        out_specs=(P("dp", "seq", None), P("dp", "seq", None), P("dp", "seq")),
        check_vma=False,
    )
```

```python
import jax
import jax.numpy as jnp
from jax import lax
from jax.experimental import pallas as pl
from jax.experimental.pallas import tpu as pltpu
from jax.sharding import PartitionSpec as P

HEADS = 16
HD = 64
BF = jnp.bfloat16
F32 = jnp.float32
ROWS = 1024
GROUP = 12


def dot(a, b, ca=1, cb=0):
    return lax.dot_general(a, b, (((ca,), (cb,)), ((), ())), preferred_element_type=F32)


def attend_kernel(
    blocks_ref, counts_ref, feat_ref, w_ref, cot_ref, ocol_ref, orow_ref,
    out_ref, gw_ref, x_ref, kv_ref, a_ref, acc_ref, g_ref, sum_ref,
):
    nodes = feat_ref.shape[0]
    clusters, slots = blocks_ref.shape
    rows = nodes // clusters
    keys = slots * rows
    tiles = nodes // ROWS
    place = (
        lax.broadcasted_iota(jnp.int32, (HD, 4 * HD), 0) + 3 * HD
        == lax.broadcasted_iota(jnp.int32, (HD, 4 * HD), 1)
    ).astype(F32).astype(BF)

    def project(i, carry):
        r = pl.ds(pl.multiple_of(i * ROWS, ROWS), ROWS)
        x = dot(feat_ref[r, :], w_ref[...]) + dot(cot_ref[r, :], place)
        x_ref[r, :] = x.astype(BF)
        return carry

    lax.fori_loop(0, tiles, project, 0)

    first = lax.broadcasted_iota(jnp.int32, (rows, 2 * HD), 1) < HD

    def to_clusters(i, carry):
        r = pl.ds(pl.multiple_of(i * ROWS, ROWS), ROWS)
        pick = ocol_ref[r, :] == lax.broadcasted_iota(jnp.int32, (ROWS, nodes), 1)
        moved = dot(pick.astype(F32).astype(BF), x_ref[...])
        kv_ref[r, :] = moved[:, : 2 * HD].astype(BF)
        for t in range(ROWS // rows):
            qd = moved[t * rows : (t + 1) * rows, 2 * HD :]
            base = pl.multiple_of(i * 2 * ROWS + 2 * rows * t, 2 * rows)
            a_ref[pl.ds(base, rows), :] = jnp.where(first, qd, 0.0).astype(BF)
            a_ref[pl.ds(base + rows, rows), :] = jnp.where(first, 0.0, qd).astype(BF)
        return carry

    lax.fori_loop(0, tiles, to_clusters, 0)

    acc_ref[...] = jnp.zeros_like(acc_ref)
    key_at = lax.broadcasted_iota(jnp.int32, (rows, keys), 1)

    def weigh(both, c):
        score = jnp.where(key_at < counts_ref[c] * rows, both[:rows], -1e30)
        dpw = both[rows:]
        raw = jnp.exp(score - jnp.max(score, axis=1, keepdims=True))
        p = raw * (1.0 / jnp.sum(raw, axis=1, keepdims=True))
        ds = p * (dpw - jnp.sum(p * dpw, axis=1, keepdims=True))
        return jnp.concatenate([ds, p], axis=0).astype(BF)

    def step(i, carry):
        group = [i * GROUP + u for u in range(GROUP)]
        ats = [
            [pl.ds(pl.multiple_of(blocks_ref[c, j] * rows, rows), rows) for j in range(slots)]
            for c in group
        ]
        kvs = [jnp.concatenate([kv_ref[s, :] for s in at], axis=0) for at in ats]
        qds = [a_ref[pl.ds(pl.multiple_of(c * 2 * rows, 2 * rows), 2 * rows), :] for c in group]
        boths = [dot(a, kv, 1, 1) for a, kv in zip(qds, kvs)]
        pds = [weigh(b, c) for b, c in zip(boths, group)]
        oqs = [dot(pd, kv) for pd, kv in zip(pds, kvs)]
        backs = [dot(pd, a, 0, 0) for pd, a in zip(pds, qds)]
        for c, oq in zip(group, oqs):
            here = pl.ds(pl.multiple_of(c * rows, rows), rows)
            g_ref[here, 2 * HD :] = jnp.where(first, oq[:rows] * 0.125, oq[rows:]).astype(BF)
        for at, back in zip(ats, backs):
            new = [acc_ref[s, :] + back[j * rows : (j + 1) * rows] for j, s in enumerate(at)]
            for s, v in zip(at, new):
                acc_ref[s, :] = v
        return carry

    lax.fori_loop(0, clusters // GROUP, step, 0)
    g_ref[:, : 2 * HD] = acc_ref[...].astype(BF)

    sum_ref[...] = jnp.zeros_like(sum_ref)

    def to_nodes(i, carry):
        r = pl.ds(pl.multiple_of(i * ROWS, ROWS), ROWS)
        pick = orow_ref[...] == lax.broadcasted_iota(jnp.int32, (ROWS, nodes), 0) + i * ROWS
        back = dot(pick.astype(F32).astype(BF), g_ref[...]).astype(BF)
        out_ref[r, :] = back
        sum_ref[...] += dot(feat_ref[r, :], back, 0, 0)
        return carry

    lax.fori_loop(0, tiles, to_nodes, 0)
    parts, tall, lanes = gw_ref.shape
    deep = tall * 2 // 3
    gw_ref[:, :deep, :] = sum_ref[:, :lanes].reshape(parts, deep, lanes).astype(BF)
    query = sum_ref[:, lanes:].reshape(parts, deep, lanes)
    low, high = query[:, : deep // 2], query[:, deep // 2 :]
    left = lax.broadcasted_iota(jnp.int32, low.shape, 2) < HD
    gw_ref[:, deep:, :] = jnp.where(left, low, pltpu.roll(high, HD, 2)).astype(BF)


def attend(feats, w_head, cot, order, blocks, counts, parts):
    nodes, width = feats.shape
    tall = width // parts * 3 // 2
    vmem = pl.BlockSpec(memory_space=pltpu.VMEM)
    smem = pl.BlockSpec(memory_space=pltpu.SMEM)
    return pl.pallas_call(
        attend_kernel,
        name="attend",
        out_shape=[
            jax.ShapeDtypeStruct((nodes, 4 * HD), BF),
            jax.ShapeDtypeStruct((parts, tall, 2 * HD), BF),
        ],
        in_specs=[smem, smem] + [vmem] * 5,
        out_specs=[vmem, vmem],
        scratch_shapes=[
            pltpu.VMEM((nodes, 4 * HD), BF),
            pltpu.VMEM((nodes, 2 * HD), BF),
            pltpu.VMEM((2 * nodes, 2 * HD), BF),
            pltpu.VMEM((nodes, 2 * HD), F32),
            pltpu.VMEM((nodes, 4 * HD), BF),
            pltpu.VMEM((width, 4 * HD), F32),
        ],
        compiler_params=pltpu.CompilerParams(vmem_limit_bytes=50 << 20),
    )(blocks, counts, feats, w_head, cot, order.reshape(nodes, 1), order.reshape(1, nodes))


def finish_kernel(g_ref, w_ref, att_ref, gf_ref, lhs_ref):
    heads = g_ref.shape[0]
    wide = heads * 2 * HD
    first = lax.broadcasted_iota(jnp.int32, (g_ref.shape[1], 2 * HD), 1) < HD
    for h in range(0, heads, 2):
        lhs_ref[:, h * 2 * HD : (h + 1) * 2 * HD] = g_ref[h, :, : 2 * HD]
        lhs_ref[:, (h + 1) * 2 * HD : (h + 2) * 2 * HD] = g_ref[h + 1, :, : 2 * HD]
        even = g_ref[h, :, 2 * HD :].astype(F32)
        odd = g_ref[h + 1, :, 2 * HD :].astype(F32)
        to = slice(h * HD, (h + 2) * HD)
        lhs_ref[:, wide + h * HD : wide + (h + 2) * HD] = jnp.where(
            first, even, pltpu.roll(odd, HD, 1)
        ).astype(BF)
        att_ref[:, to] = jnp.where(first, pltpu.roll(even, HD, 1), odd).astype(BF)
    gf_ref[...] = dot(lhs_ref[...], w_ref[...], 1, 1).astype(BF)


def finish(got, weights):
    rows, width = got.shape[1], weights.shape[0]
    vmem = pl.BlockSpec(memory_space=pltpu.VMEM)
    return pl.pallas_call(
        finish_kernel,
        name="finish",
        out_shape=[
            jax.ShapeDtypeStruct((rows, HEADS * HD), BF),
            jax.ShapeDtypeStruct((rows, width), BF),
        ],
        in_specs=[vmem, vmem],
        out_specs=[vmem, vmem],
        scratch_shapes=[pltpu.VMEM((rows, weights.shape[1]), BF)],
        compiler_params=pltpu.CompilerParams(vmem_limit_bytes=40 << 20),
    )(got, weights)


def reduce_scatter(part, axis):
    size = lax.axis_size(axis)
    me = lax.axis_index(axis)
    bit = 1
    while bit < size:
        pairs = part.reshape(-1, 2, *part.shape[1:])
        mine = lax.rem(me // bit, 2)
        keep = lax.dynamic_index_in_dim(pairs, mine, 1, keepdims=False)
        send = lax.dynamic_index_in_dim(pairs, 1 - mine, 1, keepdims=False)
        came = lax.ppermute(send, axis, [(i, i ^ bit) for i in range(size)])
        total = keep.astype(F32) + came.astype(F32)
        part = total.astype(BF)
        bit *= 2
    return total[0]


def per_device(features, qkv_weight, cotangent, node_order, blocks, counts):
    local_rows = features.shape[1]
    model_width = features.shape[2]
    deep = qkv_weight.shape[0]
    feats = features[0]
    head = lax.axis_index("seq")
    own = lax.dynamic_slice(qkv_weight, (0, head * 3 * HD), (deep, 3 * HD))
    own = jnp.concatenate(
        [own[:, HD:], own[:, :HD] * jnp.asarray(0.125, BF), jnp.zeros((deep, HD), BF)],
        axis=1,
    )
    w_head = lax.all_gather(own, "dp", axis=0, tiled=True)
    node_all = lax.all_gather(feats, "seq", axis=0, tiled=True)
    cot = lax.all_to_all(
        cotangent[0].reshape(local_rows, HEADS, HD).transpose(1, 0, 2), "seq", 0, 0, tiled=True
    ).reshape(HEADS * local_rows, HD)
    by_head = qkv_weight.reshape(deep, HEADS, 3 * HD)
    ordered = jnp.concatenate(
        [by_head[:, :, HD:].reshape(deep, -1), by_head[:, :, :HD].reshape(deep, -1)], axis=1
    )
    weights = lax.all_gather(ordered, "dp", axis=0, tiled=True)
    grads, part = attend(
        node_all, w_head, cot, node_order[0], blocks[0], counts[0], lax.axis_size("dp")
    )
    got = lax.all_to_all(grads.reshape(HEADS, local_rows, 4 * HD), "seq", 0, 0, tiled=True)
    total = reduce_scatter(part, "dp")
    query = jnp.concatenate([total[deep:, :HD], total[deep:, HD:]], axis=0)
    grad_weight = jnp.concatenate([query, total[:deep]], axis=1)
    attended, grad_feats = finish(got, weights)
    return (
        attended.reshape(1, local_rows, model_width),
        grad_feats.reshape(1, local_rows, model_width),
        grad_weight,
    )


def solution(mesh):
    return jax.shard_map(
        per_device,
        mesh=mesh,
        in_specs=(
            P("dp", "seq", None),
            P("dp", None),
            P("dp", "seq", None),
            P("dp", None),
            P("dp", None, None),
            P("dp", None),
        ),
        out_specs=(P("dp", "seq", None), P("dp", "seq", None), P("dp", "seq")),
        check_vma=False,
    )
```

```python
import jax
import jax.numpy as jnp
from jax import lax
from jax.experimental import pallas as pl
from jax.experimental.pallas import tpu as pltpu
from jax.sharding import PartitionSpec as P

HEADS = 16
HD = 64
BF = jnp.bfloat16
F32 = jnp.float32
ROWS = 1024
GROUP = 12
SIDE = 4
HOPS = (
    ((0, 0), (0, 1)), ((0, 0), (0, -1)), ((0, 0), (1, 0)), ((0, 0), (-1, 0)),
    ((1, 0), (0, 1)), ((-1, 0), (0, -1)), ((0, -1), (1, 0)), ((0, 1), (-1, 0)),
    ((0, 1), (0, 1)), ((1, -1), (0, -1)), ((1, 0), (1, 0)), ((-1, 1), (-1, 0)),
    ((2, 1), (0, 1)), ((-1, -1), (0, -1)), ((1, -1), (1, 0)),
)


SECOND = 4


def dot(a, b, ca=1, cb=0):
    return lax.dot_general(a, b, (((ca,), (cb,)), ((), ())), preferred_element_type=F32)


def attend_kernel(
    blocks_ref, counts_ref, owner_ref, ids_ref, w_ref, cot_ref, ocol_ref, orow_ref, *refs
):
    members = owner_ref.shape[0]
    parts_refs, refs = refs[:members], refs[members:]
    (out_ref, gw_ref, feat_ref, wide_ref, x_ref, kv_ref, a_ref, acc_ref, g_ref, sum_ref, sem) = refs
    nodes = feat_ref.shape[0]
    clusters, slots = blocks_ref.shape
    rows = nodes // clusters
    keys = slots * rows
    tiles = nodes // ROWS
    local = nodes // members
    loads = [
        pltpu.make_async_copy(part, feat_ref.at[pl.ds(k * local, local), :], sem.at[k])
        for k, part in enumerate(parts_refs)
    ]
    for load in loads:
        load.start()

    parts, tall, lanes = w_ref.shape
    deep = tall * 2 // 3
    width = parts * deep
    wide_ref[:, :lanes] = w_ref[:, :deep, :].reshape(width, lanes)
    packed = w_ref[:, deep:, :].astype(F32)
    left = lax.broadcasted_iota(jnp.int32, packed.shape, 2) < HD
    query = [jnp.where(left, packed, 0.0), jnp.where(left, pltpu.roll(packed, HD, 2), 0.0)]
    wide_ref[:, lanes:] = jnp.concatenate(query, axis=1).reshape(width, lanes).astype(BF)
    place = (
        lax.broadcasted_iota(jnp.int32, (HD, 4 * HD), 0) + 3 * HD
        == lax.broadcasted_iota(jnp.int32, (HD, 4 * HD), 1)
    ).astype(F32).astype(BF)

    def at_owner(k):
        return pl.ds(pl.multiple_of(owner_ref[k] * local, local), local)

    batch = 4
    for b in range(0, members, batch):
        for load in loads[b : b + batch]:
            load.wait()
        r = slice(b * local, (b + batch) * local)
        cot = jnp.concatenate([cot_ref[at_owner(b + k), :] for k in range(batch)], axis=0)
        x_ref[r, :] = (dot(feat_ref[r, :], wide_ref[...]) + dot(cot, place)).astype(BF)

    first = lax.broadcasted_iota(jnp.int32, (rows, 2 * HD), 1) < HD

    def to_clusters(i, carry):
        r = pl.ds(pl.multiple_of(i * ROWS, ROWS), ROWS)
        pick = ocol_ref[r, :] == ids_ref[...]
        moved = dot(pick.astype(F32).astype(BF), x_ref[...])
        kv_ref[r, :] = moved[:, : 2 * HD].astype(BF)
        for t in range(ROWS // rows):
            qd = moved[t * rows : (t + 1) * rows, 2 * HD :]
            base = pl.multiple_of(i * 2 * ROWS + 2 * rows * t, 2 * rows)
            a_ref[pl.ds(base, rows), :] = jnp.where(first, qd, 0.0).astype(BF)
            a_ref[pl.ds(base + rows, rows), :] = jnp.where(first, 0.0, qd).astype(BF)
        return carry

    lax.fori_loop(0, tiles, to_clusters, 0)

    acc_ref[...] = jnp.zeros_like(acc_ref)
    key_at = lax.broadcasted_iota(jnp.int32, (rows, keys), 1)

    def weigh(both, c):
        score = jnp.where(key_at < counts_ref[c] * rows, both[:rows], -1e30)
        dpw = both[rows:]
        raw = jnp.exp(score - jnp.max(score, axis=1, keepdims=True))
        p = raw * (1.0 / jnp.sum(raw, axis=1, keepdims=True))
        ds = p * (dpw - jnp.sum(p * dpw, axis=1, keepdims=True))
        return jnp.concatenate([ds, p], axis=0).astype(BF)

    def step(i, carry):
        group = [i * GROUP + u for u in range(GROUP)]
        ats = [
            [pl.ds(pl.multiple_of(blocks_ref[c, j] * rows, rows), rows) for j in range(slots)]
            for c in group
        ]
        kvs = [jnp.concatenate([kv_ref[s, :] for s in at], axis=0) for at in ats]
        qds = [a_ref[pl.ds(pl.multiple_of(c * 2 * rows, 2 * rows), 2 * rows), :] for c in group]
        boths = [dot(a, kv, 1, 1) for a, kv in zip(qds, kvs)]
        pds = [weigh(b, c) for b, c in zip(boths, group)]
        oqs = [dot(pd, kv) for pd, kv in zip(pds, kvs)]
        backs = [dot(pd, a, 0, 0) for pd, a in zip(pds, qds)]
        for c, oq in zip(group, oqs):
            here = pl.ds(pl.multiple_of(c * rows, rows), rows)
            g_ref[here, 2 * HD :] = jnp.where(first, oq[:rows] * 0.125, oq[rows:]).astype(BF)
        for at, back in zip(ats, backs):
            new = [acc_ref[s, :] + back[j * rows : (j + 1) * rows] for j, s in enumerate(at)]
            for s, v in zip(at, new):
                acc_ref[s, :] = v
        return carry

    lax.fori_loop(0, clusters // GROUP, step, 0)
    g_ref[:, : 2 * HD] = acc_ref[...].astype(BF)

    sum_ref[...] = jnp.zeros_like(sum_ref)

    half = members // 2
    here = lax.broadcasted_iota(jnp.int32, (local, nodes), 0)

    def to_nodes(i, carry):
        picks = [
            (orow_ref[...] == here + owner_ref[i * half + k] * local).astype(F32).astype(BF)
            for k in range(half)
        ]
        back = dot(jnp.concatenate(picks, axis=0), g_ref[...]).astype(BF)
        for k in range(half):
            out_ref[at_owner(i * half + k), :] = back[k * local : (k + 1) * local]
        r = pl.ds(pl.multiple_of(i * half * local, half * local), half * local)
        sum_ref[...] += dot(feat_ref[r, :], back, 0, 0)
        return carry

    lax.fori_loop(0, 2, to_nodes, 0)
    gw_ref[:, :deep, :] = sum_ref[:, :lanes].reshape(parts, deep, lanes).astype(BF)
    query = sum_ref[:, lanes:].reshape(parts, deep, lanes)
    low, high = query[:, : deep // 2], query[:, deep // 2 :]
    gw_ref[:, deep:, :] = jnp.where(left, low, pltpu.roll(high, HD, 2)).astype(BF)


def attend(blocks_of, owner, w_head, cot, order, blocks, counts):
    local, width = blocks_of[0].shape
    nodes = len(blocks_of) * local
    parts, tall, lanes = w_head.shape
    ids = (owner[:, None] * local + jnp.arange(local, dtype=jnp.int32)).reshape(1, nodes)
    vmem = pl.BlockSpec(memory_space=pltpu.VMEM)
    smem = pl.BlockSpec(memory_space=pltpu.SMEM)
    return pl.pallas_call(
        attend_kernel,
        name="attend",
        out_shape=[
            jax.ShapeDtypeStruct((nodes, 4 * HD), BF),
            jax.ShapeDtypeStruct((parts, tall, lanes), BF),
        ],
        in_specs=[smem] * 3 + [vmem] * 5 + [pl.BlockSpec(memory_space=pl.ANY)] * len(blocks_of),
        out_specs=[vmem, vmem],
        scratch_shapes=[
            pltpu.VMEM((nodes, width), BF),
            pltpu.VMEM((width, 4 * HD), BF),
            pltpu.VMEM((nodes, 4 * HD), BF),
            pltpu.VMEM((nodes, 2 * HD), BF),
            pltpu.VMEM((2 * nodes, 2 * HD), BF),
            pltpu.VMEM((nodes, 2 * HD), F32),
            pltpu.VMEM((nodes, 4 * HD), BF),
            pltpu.VMEM((width, 4 * HD), F32),
            pltpu.SemaphoreType.DMA((len(blocks_of),)),
        ],
        compiler_params=pltpu.CompilerParams(vmem_limit_bytes=52 << 20),
    )(
        blocks, counts, owner, ids, w_head, cot,
        order.reshape(nodes, 1), order.reshape(1, nodes), *blocks_of,
    )


def finish_kernel(g_ref, w_ref, att_ref, gf_ref, lhs_ref):
    heads = g_ref.shape[0]
    wide = heads * 2 * HD
    first = lax.broadcasted_iota(jnp.int32, (g_ref.shape[1], 2 * HD), 1) < HD
    for h in range(0, heads, 2):
        lhs_ref[:, h * 2 * HD : (h + 1) * 2 * HD] = g_ref[h, :, : 2 * HD]
        lhs_ref[:, (h + 1) * 2 * HD : (h + 2) * 2 * HD] = g_ref[h + 1, :, : 2 * HD]
        even = g_ref[h, :, 2 * HD :].astype(F32)
        odd = g_ref[h + 1, :, 2 * HD :].astype(F32)
        to = slice(h * HD, (h + 2) * HD)
        lhs_ref[:, wide + h * HD : wide + (h + 2) * HD] = jnp.where(
            first, even, pltpu.roll(odd, HD, 1)
        ).astype(BF)
        att_ref[:, to] = jnp.where(first, pltpu.roll(even, HD, 1), odd).astype(BF)
    gf_ref[...] = dot(lhs_ref[...], w_ref[...], 1, 1).astype(BF)


def finish(got, weights):
    rows, width = got.shape[1], weights.shape[0]
    vmem = pl.BlockSpec(memory_space=pltpu.VMEM)
    return pl.pallas_call(
        finish_kernel,
        name="finish",
        out_shape=[
            jax.ShapeDtypeStruct((rows, HEADS * HD), BF),
            jax.ShapeDtypeStruct((rows, width), BF),
        ],
        in_specs=[vmem, vmem],
        out_specs=[vmem, vmem],
        scratch_shapes=[pltpu.VMEM((rows, weights.shape[1]), BF)],
        compiler_params=pltpu.CompilerParams(vmem_limit_bytes=40 << 20),
    )(got, weights)


def reduce_scatter(part, axis):
    size = lax.axis_size(axis)
    me = lax.axis_index(axis)
    bit = 1
    while bit < size:
        pairs = part.reshape(-1, 2, *part.shape[1:])
        mine = lax.rem(me // bit, 2)
        keep = lax.dynamic_index_in_dim(pairs, mine, 1, keepdims=False)
        send = lax.dynamic_index_in_dim(pairs, 1 - mine, 1, keepdims=False)
        came = lax.ppermute(send, axis, [(i, i ^ bit) for i in range(size)])
        total = keep.astype(F32) + came.astype(F32)
        part = total.astype(BF)
        bit *= 2
    return total[0]


def gather_round(block, axis):
    y, x = lax.axis_index(axis) // SIDE, lax.rem(lax.axis_index(axis), SIDE)
    held = {(0, 0): block}
    for (hy, hx), (dy, dx) in HOPS:
        pairs = [
            ((r + dy) % SIDE * SIDE + (c + dx) % SIDE, r * SIDE + c)
            for r in range(SIDE)
            for c in range(SIDE)
        ]
        source = held[hy % SIDE, hx % SIDE]
        held[(hy + dy) % SIDE, (hx + dx) % SIDE] = lax.ppermute(source, axis, pairs)
    places = jnp.asarray(list(held), jnp.int32)
    owner = lax.rem(places[:, 0] + y, SIDE) * SIDE + lax.rem(places[:, 1] + x, SIDE)
    return list(held.values()), owner.astype(jnp.int32)


def per_device(features, qkv_weight, cotangent, node_order, blocks, counts):
    local_rows = features.shape[1]
    model_width = features.shape[2]
    deep = qkv_weight.shape[0]
    feats = features[0]
    head = lax.axis_index("seq")
    own = lax.dynamic_slice(qkv_weight, (0, head * 3 * HD), (deep, 3 * HD))
    query = own[:, :HD] * jnp.asarray(0.125, BF)
    query = jnp.concatenate([query[: deep // 2], query[deep // 2 :]], axis=1)
    own = jnp.concatenate([own[:, HD:], query], axis=0)
    copies = jnp.broadcast_to(own[None], (lax.axis_size("dp"), *own.shape))
    blocks_of, owner = gather_round(feats, "seq")
    cot = lax.all_to_all(
        cotangent[0].reshape(local_rows, HEADS, HD).transpose(1, 0, 2), "seq", 0, 0, tiled=True
    ).reshape(HEADS * local_rows, HD)
    copies, _ = lax.optimization_barrier((copies, blocks_of[SECOND]))
    w_head = lax.all_to_all(copies, "dp", 0, 0, tiled=True)
    by_head = qkv_weight.reshape(deep, HEADS, 3 * HD)
    ordered = jnp.concatenate(
        [by_head[:, :, HD:].reshape(deep, -1), by_head[:, :, :HD].reshape(deep, -1)], axis=1
    )
    weights = lax.all_gather(ordered, "dp", axis=0, tiled=True)
    grads, part = attend(blocks_of, owner, w_head, cot, node_order[0], blocks[0], counts[0])
    got = lax.all_to_all(grads.reshape(HEADS, local_rows, 4 * HD), "seq", 0, 0, tiled=True)
    total = reduce_scatter(part, "dp")
    query = jnp.concatenate([total[deep:, :HD], total[deep:, HD:]], axis=0)
    grad_weight = jnp.concatenate([query, total[:deep]], axis=1)
    attended, grad_feats = finish(got, weights)
    return (
        attended.reshape(1, local_rows, model_width),
        grad_feats.reshape(1, local_rows, model_width),
        grad_weight,
    )


def solution(mesh):
    return jax.shard_map(
        per_device,
        mesh=mesh,
        in_specs=(
            P("dp", "seq", None),
            P("dp", None),
            P("dp", "seq", None),
            P("dp", None),
            P("dp", None, None),
            P("dp", None),
        ),
        out_specs=(P("dp", "seq", None), P("dp", "seq", None), P("dp", "seq")),
        check_vma=False,
    )
```

```python
import jax
import jax.numpy as jnp
from jax import lax
from jax.experimental import pallas as pl
from jax.experimental.pallas import tpu as pltpu
from jax.sharding import PartitionSpec as P

HEADS = 16
HD = 64
BF = jnp.bfloat16
F32 = jnp.float32
ROWS = 1024
GROUP = 12
SIDE = 4
HOPS = (
    ((0, 0), (0, 1)), ((0, 0), (0, -1)), ((0, 0), (1, 0)), ((0, 0), (-1, 0)),
    ((1, 0), (0, 1)), ((-1, 0), (0, -1)), ((0, -1), (1, 0)), ((0, 1), (-1, 0)),
    ((0, 1), (0, 1)), ((1, -1), (0, -1)), ((1, 0), (1, 0)), ((-1, 1), (-1, 0)),
    ((2, 1), (0, 1)), ((-1, -1), (0, -1)), ((1, -1), (1, 0)),
)


def dot(a, b, ca=1, cb=0):
    return lax.dot_general(a, b, (((ca,), (cb,)), ((), ())), preferred_element_type=F32)


def attend_kernel(
    blocks_ref, counts_ref, owner_ref, head_ref, ids_ref, cot_ref, ocol_ref, orow_ref, w_ref, *refs
):
    members = owner_ref.shape[0]
    parts_refs, refs = refs[:members], refs[members:]
    (out_ref, gw_ref, feat_ref, wide_ref, pair_ref, x_ref, kv_ref, a_ref, acc_ref, g_ref, sum_ref, sem) = refs
    nodes = feat_ref.shape[0]
    clusters, slots = blocks_ref.shape
    rows = nodes // clusters
    keys = slots * rows
    tiles = nodes // ROWS
    local = nodes // members
    loads = [
        pltpu.make_async_copy(part, feat_ref.at[pl.ds(k * local, local), :], sem.at[k])
        for k, part in enumerate(parts_refs)
    ]
    parts, tall, lanes = gw_ref.shape
    deep = tall * 2 // 3
    head = head_ref[0]
    key_at = pl.multiple_of(head * lanes, lanes)
    query_at = pl.multiple_of((HEADS + head // 2) * lanes, lanes)
    weigh_in = [
        pltpu.make_async_copy(
            w_ref.at[:, pl.ds(key_at, lanes)], wide_ref.at[:, pl.ds(0, lanes)], sem.at[members]
        ),
        pltpu.make_async_copy(w_ref.at[:, pl.ds(query_at, lanes)], pair_ref, sem.at[members + 1]),
    ]
    for load in weigh_in + loads:
        load.start()
    for load in weigh_in:
        load.wait()
    two = pair_ref[...].astype(F32)
    mine = jnp.where(lax.rem(head, 2) == 0, two, pltpu.roll(two, HD, 1))
    left = lax.broadcasted_iota(jnp.int32, two.shape, 1) < HD
    wide_ref[:, lanes:] = jnp.where(left, mine * 0.125, 0.0).astype(BF)
    place = (
        lax.broadcasted_iota(jnp.int32, (HD, 4 * HD), 0) + 3 * HD
        == lax.broadcasted_iota(jnp.int32, (HD, 4 * HD), 1)
    ).astype(F32).astype(BF)

    def at_owner(k):
        return pl.ds(pl.multiple_of(owner_ref[k] * local, local), local)

    batch = 4
    for b in range(0, members, batch):
        for load in loads[b : b + batch]:
            load.wait()
        r = slice(b * local, (b + batch) * local)
        cot = jnp.concatenate([cot_ref[at_owner(b + k), :] for k in range(batch)], axis=0)
        x_ref[r, :] = (dot(feat_ref[r, :], wide_ref[...]) + dot(cot, place)).astype(BF)

    first = lax.broadcasted_iota(jnp.int32, (rows, 2 * HD), 1) < HD

    def to_clusters(i, carry):
        r = pl.ds(pl.multiple_of(i * ROWS, ROWS), ROWS)
        pick = ocol_ref[r, :] == ids_ref[...]
        moved = dot(pick.astype(F32).astype(BF), x_ref[...])
        kv_ref[r, :] = moved[:, : 2 * HD].astype(BF)
        for t in range(ROWS // rows):
            qd = moved[t * rows : (t + 1) * rows, 2 * HD :]
            base = pl.multiple_of(i * 2 * ROWS + 2 * rows * t, 2 * rows)
            a_ref[pl.ds(base, rows), :] = jnp.where(first, qd, 0.0).astype(BF)
            a_ref[pl.ds(base + rows, rows), :] = jnp.where(first, 0.0, qd).astype(BF)
        return carry

    lax.fori_loop(0, tiles, to_clusters, 0)

    acc_ref[...] = jnp.zeros_like(acc_ref)
    place_of = lax.broadcasted_iota(jnp.int32, (rows, keys), 1)

    def weigh(both, c):
        score = jnp.where(place_of < counts_ref[c] * rows, both[:rows], -1e30)
        dpw = both[rows:]
        raw = jnp.exp(score - jnp.max(score, axis=1, keepdims=True))
        p = raw * (1.0 / jnp.sum(raw, axis=1, keepdims=True))
        ds = p * (dpw - jnp.sum(p * dpw, axis=1, keepdims=True))
        return jnp.concatenate([ds, p], axis=0).astype(BF)

    def step(i, carry):
        group = [i * GROUP + u for u in range(GROUP)]
        ats = [
            [pl.ds(pl.multiple_of(blocks_ref[c, j] * rows, rows), rows) for j in range(slots)]
            for c in group
        ]
        kvs = [jnp.concatenate([kv_ref[s, :] for s in at], axis=0) for at in ats]
        qds = [a_ref[pl.ds(pl.multiple_of(c * 2 * rows, 2 * rows), 2 * rows), :] for c in group]
        boths = [dot(a, kv, 1, 1) for a, kv in zip(qds, kvs)]
        pds = [weigh(b, c) for b, c in zip(boths, group)]
        oqs = [dot(pd, kv) for pd, kv in zip(pds, kvs)]
        backs = [dot(pd, a, 0, 0) for pd, a in zip(pds, qds)]
        for c, oq in zip(group, oqs):
            here = pl.ds(pl.multiple_of(c * rows, rows), rows)
            g_ref[here, 2 * HD :] = jnp.where(first, oq[:rows] * 0.125, oq[rows:]).astype(BF)
        for at, back in zip(ats, backs):
            new = [acc_ref[s, :] + back[j * rows : (j + 1) * rows] for j, s in enumerate(at)]
            for s, v in zip(at, new):
                acc_ref[s, :] = v
        return carry

    lax.fori_loop(0, clusters // GROUP, step, 0)
    g_ref[:, : 2 * HD] = acc_ref[...].astype(BF)

    sum_ref[...] = jnp.zeros_like(sum_ref)

    half = members // 2
    here = lax.broadcasted_iota(jnp.int32, (local, nodes), 0)

    def to_nodes(i, carry):
        picks = [
            (orow_ref[...] == here + owner_ref[i * half + k] * local).astype(F32).astype(BF)
            for k in range(half)
        ]
        back = dot(jnp.concatenate(picks, axis=0), g_ref[...]).astype(BF)
        for k in range(half):
            out_ref[at_owner(i * half + k), :] = back[k * local : (k + 1) * local]
        r = pl.ds(pl.multiple_of(i * half * local, half * local), half * local)
        sum_ref[...] += dot(feat_ref[r, :], back, 0, 0)
        return carry

    lax.fori_loop(0, 2, to_nodes, 0)
    gw_ref[:, :deep, :] = sum_ref[:, :lanes].reshape(parts, deep, lanes).astype(BF)
    query = sum_ref[:, lanes:].reshape(parts, deep, lanes)
    low, high = query[:, : deep // 2], query[:, deep // 2 :]
    left = lax.broadcasted_iota(jnp.int32, low.shape, 2) < HD
    gw_ref[:, deep:, :] = jnp.where(left, low, pltpu.roll(high, HD, 2)).astype(BF)


def attend(blocks_of, owner, head, weights, cot, order, blocks, counts, parts):
    local, width = blocks_of[0].shape
    nodes = len(blocks_of) * local
    tall, lanes = width // parts * 3 // 2, 2 * HD
    ids = (owner[:, None] * local + jnp.arange(local, dtype=jnp.int32)).reshape(1, nodes)
    vmem = pl.BlockSpec(memory_space=pltpu.VMEM)
    smem = pl.BlockSpec(memory_space=pltpu.SMEM)
    return pl.pallas_call(
        attend_kernel,
        name="attend",
        out_shape=[
            jax.ShapeDtypeStruct((nodes, 4 * HD), BF),
            jax.ShapeDtypeStruct((parts, tall, lanes), BF),
        ],
        in_specs=[smem] * 4
        + [vmem] * 4
        + [pl.BlockSpec(memory_space=pl.ANY)] * (1 + len(blocks_of)),
        out_specs=[vmem, vmem],
        scratch_shapes=[
            pltpu.VMEM((nodes, width), BF),
            pltpu.VMEM((width, 4 * HD), BF),
            pltpu.VMEM((width, 2 * HD), BF),
            pltpu.VMEM((nodes, 4 * HD), BF),
            pltpu.VMEM((nodes, 2 * HD), BF),
            pltpu.VMEM((2 * nodes, 2 * HD), BF),
            pltpu.VMEM((nodes, 2 * HD), F32),
            pltpu.VMEM((nodes, 4 * HD), BF),
            pltpu.VMEM((width, 4 * HD), F32),
            pltpu.SemaphoreType.DMA((len(blocks_of) + 2,)),
        ],
        compiler_params=pltpu.CompilerParams(vmem_limit_bytes=52 << 20),
    )(
        blocks, counts, owner, head.reshape(1), ids, cot,
        order.reshape(nodes, 1), order.reshape(1, nodes), weights, *blocks_of,
    )


def finish_kernel(g_ref, w_ref, att_ref, gf_ref, lhs_ref, have_ref, sem):
    bands = sem.shape[0]
    band = w_ref.shape[0] // bands
    cuts = [slice(i * band, (i + 1) * band) for i in range(bands)]
    loads = [
        pltpu.make_async_copy(w_ref.at[cut, :], have_ref.at[cut, :], sem.at[i])
        for i, cut in enumerate(cuts)
    ]
    for load in loads:
        load.start()
    heads = g_ref.shape[0]
    wide = heads * 2 * HD
    first = lax.broadcasted_iota(jnp.int32, (g_ref.shape[1], 2 * HD), 1) < HD
    for h in range(0, heads, 2):
        lhs_ref[:, h * 2 * HD : (h + 1) * 2 * HD] = g_ref[h, :, : 2 * HD]
        lhs_ref[:, (h + 1) * 2 * HD : (h + 2) * 2 * HD] = g_ref[h + 1, :, : 2 * HD]
        even = g_ref[h, :, 2 * HD :].astype(F32)
        odd = g_ref[h + 1, :, 2 * HD :].astype(F32)
        to = slice(h * HD, (h + 2) * HD)
        lhs_ref[:, wide + h * HD : wide + (h + 2) * HD] = jnp.where(
            first, even, pltpu.roll(odd, HD, 1)
        ).astype(BF)
        att_ref[:, to] = jnp.where(first, pltpu.roll(even, HD, 1), odd).astype(BF)
    for cut, load in zip(cuts, loads):
        load.wait()
        gf_ref[:, cut] = dot(lhs_ref[...], have_ref[cut, :], 1, 1).astype(BF)


def finish(got, weights):
    rows, width = got.shape[1], weights.shape[0]
    vmem = pl.BlockSpec(memory_space=pltpu.VMEM)
    return pl.pallas_call(
        finish_kernel,
        name="finish",
        out_shape=[
            jax.ShapeDtypeStruct((rows, HEADS * HD), BF),
            jax.ShapeDtypeStruct((rows, width), BF),
        ],
        in_specs=[vmem, pl.BlockSpec(memory_space=pl.ANY)],
        out_specs=[vmem, vmem],
        scratch_shapes=[
            pltpu.VMEM((rows, weights.shape[1]), BF),
            pltpu.VMEM(weights.shape, BF),
            pltpu.SemaphoreType.DMA((4,)),
        ],
        compiler_params=pltpu.CompilerParams(vmem_limit_bytes=40 << 20),
    )(got, weights)


def reduce_scatter(part, axis):
    size = lax.axis_size(axis)
    me = lax.axis_index(axis)
    bit = 1
    while bit < size:
        pairs = part.reshape(-1, 2, *part.shape[1:])
        mine = lax.rem(me // bit, 2)
        keep = lax.dynamic_index_in_dim(pairs, mine, 1, keepdims=False)
        send = lax.dynamic_index_in_dim(pairs, 1 - mine, 1, keepdims=False)
        came = lax.ppermute(send, axis, [(i, i ^ bit) for i in range(size)])
        total = keep.astype(F32) + came.astype(F32)
        part = total.astype(BF)
        bit *= 2
    return total[0]


def gather_round(block, axis):
    y, x = lax.axis_index(axis) // SIDE, lax.rem(lax.axis_index(axis), SIDE)
    held = {(0, 0): block}
    for (hy, hx), (dy, dx) in HOPS:
        pairs = [
            ((r + dy) % SIDE * SIDE + (c + dx) % SIDE, r * SIDE + c)
            for r in range(SIDE)
            for c in range(SIDE)
        ]
        source = held[hy % SIDE, hx % SIDE]
        held[(hy + dy) % SIDE, (hx + dx) % SIDE] = lax.ppermute(source, axis, pairs)
    places = jnp.asarray(list(held), jnp.int32)
    owner = lax.rem(places[:, 0] + y, SIDE) * SIDE + lax.rem(places[:, 1] + x, SIDE)
    return list(held.values()), owner.astype(jnp.int32)


def per_device(features, qkv_weight, cotangent, node_order, blocks, counts):
    local_rows = features.shape[1]
    model_width = features.shape[2]
    deep = qkv_weight.shape[0]
    feats = features[0]
    head = lax.axis_index("seq")
    by_head = qkv_weight.reshape(deep, HEADS, 3 * HD)
    ordered = jnp.concatenate(
        [by_head[:, :, HD:].reshape(deep, -1), by_head[:, :, :HD].reshape(deep, -1)], axis=1
    )
    size = lax.axis_size("dp")
    core = lax.rem(lax.axis_index("dp"), 2)
    other = lax.ppermute(ordered, "dp", [(i, i ^ 1) for i in range(size)])
    chip = jnp.where(
        core == 0, jnp.stack([ordered, other]), jnp.stack([other, ordered])
    ).reshape(2 * deep, -1)
    groups = [list(range(c, size, 2)) for c in range(2)]
    weights = lax.all_gather(chip, "dp", axis=0, tiled=True, axis_index_groups=groups)
    blocks_of, owner = gather_round(feats, "seq")
    cot = lax.all_to_all(
        cotangent[0].reshape(local_rows, HEADS, HD).transpose(1, 0, 2), "seq", 0, 0, tiled=True
    ).reshape(HEADS * local_rows, HD)
    grads, part = attend(
        blocks_of, owner, head, weights, cot, node_order[0], blocks[0], counts[0], size
    )
    got = lax.all_to_all(grads.reshape(HEADS, local_rows, 4 * HD), "seq", 0, 0, tiled=True)
    total = reduce_scatter(part, "dp")
    query = jnp.concatenate([total[deep:, :HD], total[deep:, HD:]], axis=0)
    grad_weight = jnp.concatenate([query, total[:deep]], axis=1)
    attended, grad_feats = finish(got, weights)
    return (
        attended.reshape(1, local_rows, model_width),
        grad_feats.reshape(1, local_rows, model_width),
        grad_weight,
    )


def solution(mesh):
    return jax.shard_map(
        per_device,
        mesh=mesh,
        in_specs=(
            P("dp", "seq", None),
            P("dp", None),
            P("dp", "seq", None),
            P("dp", None),
            P("dp", None, None),
            P("dp", None),
        ),
        out_specs=(P("dp", "seq", None), P("dp", "seq", None), P("dp", "seq")),
        check_vma=False,
    )
```

```python
import jax
import jax.numpy as jnp
from jax import lax
from jax.experimental import pallas as pl
from jax.experimental.pallas import tpu as pltpu
from jax.sharding import PartitionSpec as P

HEADS = 16
HD = 64
BF = jnp.bfloat16
F32 = jnp.float32
ROWS = 1024
GROUP = 12
SIDE = 4
HOPS = (
    ((0, 0), (0, 1)), ((0, 0), (0, -1)), ((0, 0), (1, 0)), ((0, 0), (-1, 0)),
    ((1, 0), (0, 1)), ((-1, 0), (0, -1)), ((0, -1), (1, 0)), ((0, 1), (-1, 0)),
    ((0, 1), (0, 1)), ((1, -1), (0, -1)), ((1, 0), (1, 0)), ((-1, 1), (-1, 0)),
    ((2, 1), (0, 1)), ((-1, -1), (0, -1)), ((1, -1), (1, 0)),
)


def dot(a, b, ca=1, cb=0):
    return lax.dot_general(a, b, (((ca,), (cb,)), ((), ())), preferred_element_type=F32)


def attend_kernel(
    blocks_ref, counts_ref, owner_ref, ids_ref, w_ref, cot_ref, ocol_ref, orow_ref, *refs
):
    members = owner_ref.shape[0]
    parts_refs, refs = refs[:members], refs[members:]
    (out_ref, gw_ref, feat_ref, wide_ref, x_ref, kv_ref, a_ref, acc_ref, g_ref, sum_ref, sem) = refs
    nodes = feat_ref.shape[0]
    clusters, slots = blocks_ref.shape
    rows = nodes // clusters
    keys = slots * rows
    tiles = nodes // ROWS
    local = nodes // members
    loads = [
        pltpu.make_async_copy(part, feat_ref.at[pl.ds(k * local, local), :], sem.at[k])
        for k, part in enumerate(parts_refs)
    ]
    for load in loads:
        load.start()

    chips, tall, lanes = w_ref.shape
    deep = tall * 2 // 3
    wide_ref[:, :lanes] = w_ref[:, :deep, :].reshape(chips * deep, lanes)
    packed = w_ref[:, deep:, :].astype(F32)
    left = lax.broadcasted_iota(jnp.int32, packed.shape, 2) < HD
    query = [jnp.where(left, packed, 0.0), jnp.where(left, pltpu.roll(packed, HD, 2), 0.0)]
    wide_ref[:, lanes:] = jnp.concatenate(query, axis=1).reshape(chips * deep, lanes).astype(BF)
    place = (
        lax.broadcasted_iota(jnp.int32, (HD, 4 * HD), 0) + 3 * HD
        == lax.broadcasted_iota(jnp.int32, (HD, 4 * HD), 1)
    ).astype(F32).astype(BF)

    def at_owner(k):
        return pl.ds(pl.multiple_of(owner_ref[k] * local, local), local)

    batch = 4
    for b in range(0, members, batch):
        for load in loads[b : b + batch]:
            load.wait()
        r = slice(b * local, (b + batch) * local)
        cot = jnp.concatenate([cot_ref[at_owner(b + k), :] for k in range(batch)], axis=0)
        x_ref[r, :] = (dot(feat_ref[r, :], wide_ref[...]) + dot(cot, place)).astype(BF)

    first = lax.broadcasted_iota(jnp.int32, (rows, 2 * HD), 1) < HD

    def to_clusters(i, carry):
        r = pl.ds(pl.multiple_of(i * ROWS, ROWS), ROWS)
        pick = ocol_ref[r, :] == ids_ref[...]
        moved = dot(pick.astype(F32).astype(BF), x_ref[...])
        kv_ref[r, :] = moved[:, : 2 * HD].astype(BF)
        for t in range(ROWS // rows):
            qd = moved[t * rows : (t + 1) * rows, 2 * HD :]
            base = pl.multiple_of(i * 2 * ROWS + 2 * rows * t, 2 * rows)
            a_ref[pl.ds(base, rows), :] = jnp.where(first, qd, 0.0).astype(BF)
            a_ref[pl.ds(base + rows, rows), :] = jnp.where(first, 0.0, qd).astype(BF)
        return carry

    lax.fori_loop(0, tiles, to_clusters, 0)

    acc_ref[...] = jnp.zeros_like(acc_ref)
    place_of = lax.broadcasted_iota(jnp.int32, (rows, keys), 1)

    def weigh(both, c):
        score = jnp.where(place_of < counts_ref[c] * rows, both[:rows], -1e30)
        dpw = both[rows:]
        raw = jnp.exp(score - jnp.max(score, axis=1, keepdims=True))
        p = raw * (1.0 / jnp.sum(raw, axis=1, keepdims=True))
        ds = p * (dpw - jnp.sum(p * dpw, axis=1, keepdims=True))
        return jnp.concatenate([ds, p], axis=0).astype(BF)

    def step(i, carry):
        group = [i * GROUP + u for u in range(GROUP)]
        ats = [
            [pl.ds(pl.multiple_of(blocks_ref[c, j] * rows, rows), rows) for j in range(slots)]
            for c in group
        ]
        kvs = [jnp.concatenate([kv_ref[s, :] for s in at], axis=0) for at in ats]
        qds = [a_ref[pl.ds(pl.multiple_of(c * 2 * rows, 2 * rows), 2 * rows), :] for c in group]
        boths = [dot(a, kv, 1, 1) for a, kv in zip(qds, kvs)]
        pds = [weigh(b, c) for b, c in zip(boths, group)]
        oqs = [dot(pd, kv) for pd, kv in zip(pds, kvs)]
        backs = [dot(pd, a, 0, 0) for pd, a in zip(pds, qds)]
        for c, oq in zip(group, oqs):
            here = pl.ds(pl.multiple_of(c * rows, rows), rows)
            g_ref[here, 2 * HD :] = jnp.where(first, oq[:rows] * 0.125, oq[rows:]).astype(BF)
        for at, back in zip(ats, backs):
            new = [acc_ref[s, :] + back[j * rows : (j + 1) * rows] for j, s in enumerate(at)]
            for s, v in zip(at, new):
                acc_ref[s, :] = v
        return carry

    lax.fori_loop(0, clusters // GROUP, step, 0)
    g_ref[:, : 2 * HD] = acc_ref[...].astype(BF)

    sum_ref[...] = jnp.zeros_like(sum_ref)

    half = members // 2
    here = lax.broadcasted_iota(jnp.int32, (local, nodes), 0)

    def to_nodes(i, carry):
        picks = [
            (orow_ref[...] == here + owner_ref[i * half + k] * local).astype(F32).astype(BF)
            for k in range(half)
        ]
        back = dot(jnp.concatenate(picks, axis=0), g_ref[...]).astype(BF)
        for k in range(half):
            out_ref[at_owner(i * half + k), :] = back[k * local : (k + 1) * local]
        r = pl.ds(pl.multiple_of(i * half * local, half * local), half * local)
        sum_ref[...] += dot(feat_ref[r, :], back, 0, 0)
        return carry

    lax.fori_loop(0, 2, to_nodes, 0)
    parts, tall, lanes = gw_ref.shape
    deep = tall * 2 // 3
    gw_ref[:, :deep, :] = sum_ref[:, :lanes].reshape(parts, deep, lanes).astype(BF)
    query = sum_ref[:, lanes:].reshape(parts, deep, lanes)
    low, high = query[:, : deep // 2], query[:, deep // 2 :]
    left = lax.broadcasted_iota(jnp.int32, low.shape, 2) < HD
    gw_ref[:, deep:, :] = jnp.where(left, low, pltpu.roll(high, HD, 2)).astype(BF)


def attend(blocks_of, owner, w_head, cot, order, blocks, counts, parts):
    local, width = blocks_of[0].shape
    nodes = len(blocks_of) * local
    tall, lanes = width // parts * 3 // 2, 2 * HD
    ids = (owner[:, None] * local + jnp.arange(local, dtype=jnp.int32)).reshape(1, nodes)
    vmem = pl.BlockSpec(memory_space=pltpu.VMEM)
    smem = pl.BlockSpec(memory_space=pltpu.SMEM)
    return pl.pallas_call(
        attend_kernel,
        name="attend",
        out_shape=[
            jax.ShapeDtypeStruct((nodes, 4 * HD), BF),
            jax.ShapeDtypeStruct((parts, tall, lanes), BF),
        ],
        in_specs=[smem] * 3 + [vmem] * 5 + [pl.BlockSpec(memory_space=pl.ANY)] * len(blocks_of),
        out_specs=[vmem, vmem],
        scratch_shapes=[
            pltpu.VMEM((nodes, width), BF),
            pltpu.VMEM((width, 4 * HD), BF),
            pltpu.VMEM((nodes, 4 * HD), BF),
            pltpu.VMEM((nodes, 2 * HD), BF),
            pltpu.VMEM((2 * nodes, 2 * HD), BF),
            pltpu.VMEM((nodes, 2 * HD), F32),
            pltpu.VMEM((nodes, 4 * HD), BF),
            pltpu.VMEM((width, 4 * HD), F32),
            pltpu.SemaphoreType.DMA((len(blocks_of),)),
        ],
        compiler_params=pltpu.CompilerParams(vmem_limit_bytes=52 << 20),
    )(
        blocks, counts, owner, ids, w_head, cot,
        order.reshape(nodes, 1), order.reshape(1, nodes), *blocks_of,
    )


def finish_kernel(g_ref, w_ref, att_ref, gf_ref, lhs_ref):
    heads = g_ref.shape[0]
    wide = heads * 2 * HD
    first = lax.broadcasted_iota(jnp.int32, (g_ref.shape[1], 2 * HD), 1) < HD
    for h in range(0, heads, 2):
        lhs_ref[:, h * 2 * HD : (h + 1) * 2 * HD] = g_ref[h, :, : 2 * HD]
        lhs_ref[:, (h + 1) * 2 * HD : (h + 2) * 2 * HD] = g_ref[h + 1, :, : 2 * HD]
        even = g_ref[h, :, 2 * HD :].astype(F32)
        odd = g_ref[h + 1, :, 2 * HD :].astype(F32)
        to = slice(h * HD, (h + 2) * HD)
        lhs_ref[:, wide + h * HD : wide + (h + 2) * HD] = jnp.where(
            first, even, pltpu.roll(odd, HD, 1)
        ).astype(BF)
        att_ref[:, to] = jnp.where(first, pltpu.roll(even, HD, 1), odd).astype(BF)
    gf_ref[...] = dot(lhs_ref[...], w_ref[...], 1, 1).astype(BF)


def finish(got, weights):
    rows, width = got.shape[1], weights.shape[0]
    vmem = pl.BlockSpec(memory_space=pltpu.VMEM)
    return pl.pallas_call(
        finish_kernel,
        name="finish",
        out_shape=[
            jax.ShapeDtypeStruct((rows, HEADS * HD), BF),
            jax.ShapeDtypeStruct((rows, width), BF),
        ],
        in_specs=[vmem, vmem],
        out_specs=[vmem, vmem],
        scratch_shapes=[pltpu.VMEM((rows, weights.shape[1]), BF)],
        compiler_params=pltpu.CompilerParams(vmem_limit_bytes=40 << 20),
    )(got, weights)


def reduce_scatter(part, axis, got, weights):
    size = lax.axis_size(axis)
    me = lax.axis_index(axis)
    bit = 1
    while bit < size:
        pairs = part.reshape(-1, 2, *part.shape[1:])
        mine = lax.rem(me // bit, 2)
        keep = lax.dynamic_index_in_dim(pairs, mine, 1, keepdims=False)
        send = lax.dynamic_index_in_dim(pairs, 1 - mine, 1, keepdims=False)
        if 2 * bit == size:
            send, got = lax.optimization_barrier((send, got))
        came = lax.ppermute(send, axis, [(i, i ^ bit) for i in range(size)])
        if 2 * bit == size:
            came, *done = lax.optimization_barrier((came, *finish(got, weights)))
        total = keep.astype(F32) + came.astype(F32)
        part = total.astype(BF)
        bit *= 2
    return total[0], done


def gather_round(block, axis):
    y, x = lax.axis_index(axis) // SIDE, lax.rem(lax.axis_index(axis), SIDE)
    held = {(0, 0): block}
    for (hy, hx), (dy, dx) in HOPS:
        pairs = [
            ((r + dy) % SIDE * SIDE + (c + dx) % SIDE, r * SIDE + c)
            for r in range(SIDE)
            for c in range(SIDE)
        ]
        source = held[hy % SIDE, hx % SIDE]
        held[(hy + dy) % SIDE, (hx + dx) % SIDE] = lax.ppermute(source, axis, pairs)
    places = jnp.asarray(list(held), jnp.int32)
    owner = lax.rem(places[:, 0] + y, SIDE) * SIDE + lax.rem(places[:, 1] + x, SIDE)
    return list(held.values()), owner.astype(jnp.int32)


def per_device(features, qkv_weight, cotangent, node_order, blocks, counts):
    local_rows = features.shape[1]
    model_width = features.shape[2]
    deep = qkv_weight.shape[0]
    feats = features[0]
    head = lax.axis_index("seq")
    by_head = qkv_weight.reshape(deep, HEADS, 3 * HD)
    ordered = jnp.concatenate(
        [by_head[:, :, HD:].reshape(deep, -1), by_head[:, :, :HD].reshape(deep, -1)], axis=1
    )
    size = lax.axis_size("dp")
    core = lax.rem(lax.axis_index("dp"), 2)
    other = lax.ppermute(ordered, "dp", [(i, i ^ 1) for i in range(size)])
    chip = jnp.where(
        core == 0, jnp.stack([ordered, other]), jnp.stack([other, ordered])
    ).reshape(2 * deep, -1)
    groups = [list(range(c, size, 2)) for c in range(2)]
    weights = lax.all_gather(chip, "dp", axis=0, tiled=True, axis_index_groups=groups)
    own = lax.dynamic_slice(chip, (0, head * 2 * HD), (2 * deep, 2 * HD))
    query = lax.dynamic_slice(chip, (0, (2 * HEADS + head) * HD), (2 * deep, HD))
    query = query * jnp.asarray(0.125, BF)
    own = jnp.concatenate(
        [own, jnp.concatenate([query[:deep], query[deep:]], axis=1)], axis=0
    )
    copies = jnp.broadcast_to(own[None], (size // 2, *own.shape))
    w_head = lax.all_to_all(copies, "dp", 0, 0, tiled=True, axis_index_groups=groups)
    blocks_of, owner = gather_round(feats, "seq")
    by_owner = cotangent[0].reshape(local_rows, HEADS, HD).transpose(1, 0, 2)
    by_owner, w_head = lax.optimization_barrier((by_owner, w_head))
    cot = lax.all_to_all(by_owner, "seq", 0, 0, tiled=True).reshape(HEADS * local_rows, HD)
    grads, part = attend(
        blocks_of, owner, w_head, cot, node_order[0], blocks[0], counts[0], size
    )
    got = lax.all_to_all(grads.reshape(HEADS, local_rows, 4 * HD), "seq", 0, 0, tiled=True)
    total, (attended, grad_feats) = reduce_scatter(part, "dp", got, weights)
    query = jnp.concatenate([total[deep:, :HD], total[deep:, HD:]], axis=0)
    grad_weight = jnp.concatenate([query, total[:deep]], axis=1)
    return (
        attended.reshape(1, local_rows, model_width),
        grad_feats.reshape(1, local_rows, model_width),
        grad_weight,
    )


def solution(mesh):
    return jax.shard_map(
        per_device,
        mesh=mesh,
        in_specs=(
            P("dp", "seq", None),
            P("dp", None),
            P("dp", "seq", None),
            P("dp", None),
            P("dp", None, None),
            P("dp", None),
        ),
        out_specs=(P("dp", "seq", None), P("dp", "seq", None), P("dp", "seq")),
        check_vma=False,
    )
```

```python
import jax
import jax.numpy as jnp
from jax import lax
from jax.experimental import pallas as pl
from jax.experimental.pallas import tpu as pltpu
from jax.sharding import PartitionSpec as P

HEADS = 16
HD = 64
BF = jnp.bfloat16
F32 = jnp.float32
ROWS = 1024
GROUP = 12
SIDE = 4
HOPS = (
    ((0, 0), (0, 1)), ((0, 0), (0, -1)), ((0, 0), (1, 0)), ((0, 0), (-1, 0)),
    ((1, 0), (0, 1)), ((-1, 0), (0, -1)), ((0, -1), (1, 0)), ((0, 1), (-1, 0)),
    ((0, 1), (0, 1)), ((1, -1), (0, -1)), ((1, 0), (1, 0)), ((-1, 1), (-1, 0)),
    ((2, 1), (0, 1)), ((-1, -1), (0, -1)), ((1, -1), (1, 0)),
)


def dot(a, b, ca=1, cb=0):
    return lax.dot_general(a, b, (((ca,), (cb,)), ((), ())), preferred_element_type=F32)


def attend_kernel(
    blocks_ref, counts_ref, owner_ref, ids_ref, w_ref, cot_ref, ocol_ref, orow_ref, rest_ref, *refs
):
    members = owner_ref.shape[0]
    parts_refs, refs = refs[:members], refs[members:]
    (out_ref, gw_ref, feat_ref, wide_ref, x_ref, kv_ref, a_ref, acc_ref, g_ref, sum_ref, sem) = refs
    nodes = feat_ref.shape[0]
    clusters, slots = blocks_ref.shape
    rows = nodes // clusters
    keys = slots * rows
    tiles = nodes // ROWS
    local = nodes // members
    near = parts_refs[0].shape[1]
    far = rest_ref.shape[1]

    def at_owner(k):
        return pl.ds(pl.multiple_of(owner_ref[k] * local, local), local)

    loads = []
    for k, part in enumerate(parts_refs):
        to = pl.ds(k * local, local)
        loads += [
            pltpu.make_async_copy(part, feat_ref.at[to, pl.ds(0, near)], sem.at[2 * k]),
            pltpu.make_async_copy(
                rest_ref.at[at_owner(k), :], feat_ref.at[to, pl.ds(near, far)], sem.at[2 * k + 1]
            ),
        ]
    for load in loads:
        load.start()

    chips, tall, lanes = w_ref.shape
    deep = tall * 2 // 3
    wide_ref[:, :lanes] = w_ref[:, :deep, :].reshape(chips * deep, lanes)
    packed = w_ref[:, deep:, :].astype(F32)
    left = lax.broadcasted_iota(jnp.int32, packed.shape, 2) < HD
    query = [jnp.where(left, packed, 0.0), jnp.where(left, pltpu.roll(packed, HD, 2), 0.0)]
    wide_ref[:, lanes:] = jnp.concatenate(query, axis=1).reshape(chips * deep, lanes).astype(BF)
    place = (
        lax.broadcasted_iota(jnp.int32, (HD, 4 * HD), 0) + 3 * HD
        == lax.broadcasted_iota(jnp.int32, (HD, 4 * HD), 1)
    ).astype(F32).astype(BF)

    batch = 4
    for b in range(0, members, batch):
        for load in loads[2 * b : 2 * (b + batch)]:
            load.wait()
        r = slice(b * local, (b + batch) * local)
        cot = jnp.concatenate([cot_ref[at_owner(b + k), :] for k in range(batch)], axis=0)
        x_ref[r, :] = (dot(feat_ref[r, :], wide_ref[...]) + dot(cot, place)).astype(BF)

    first = lax.broadcasted_iota(jnp.int32, (rows, 2 * HD), 1) < HD

    def to_clusters(i, carry):
        r = pl.ds(pl.multiple_of(i * ROWS, ROWS), ROWS)
        pick = ocol_ref[r, :] == ids_ref[...]
        moved = dot(pick.astype(F32).astype(BF), x_ref[...])
        kv_ref[r, :] = moved[:, : 2 * HD].astype(BF)
        for t in range(ROWS // rows):
            qd = moved[t * rows : (t + 1) * rows, 2 * HD :]
            base = pl.multiple_of(i * 2 * ROWS + 2 * rows * t, 2 * rows)
            a_ref[pl.ds(base, rows), :] = jnp.where(first, qd, 0.0).astype(BF)
            a_ref[pl.ds(base + rows, rows), :] = jnp.where(first, 0.0, qd).astype(BF)
        return carry

    lax.fori_loop(0, tiles, to_clusters, 0)

    acc_ref[...] = jnp.zeros_like(acc_ref)
    place_of = lax.broadcasted_iota(jnp.int32, (rows, keys), 1)

    def weigh(both, c):
        score = jnp.where(place_of < counts_ref[c] * rows, both[:rows], -1e30)
        dpw = both[rows:]
        raw = jnp.exp(score - jnp.max(score, axis=1, keepdims=True))
        p = raw * (1.0 / jnp.sum(raw, axis=1, keepdims=True))
        ds = p * (dpw - jnp.sum(p * dpw, axis=1, keepdims=True))
        return jnp.concatenate([ds, p], axis=0).astype(BF)

    def step(i, carry):
        group = [i * GROUP + u for u in range(GROUP)]
        ats = [
            [pl.ds(pl.multiple_of(blocks_ref[c, j] * rows, rows), rows) for j in range(slots)]
            for c in group
        ]
        kvs = [jnp.concatenate([kv_ref[s, :] for s in at], axis=0) for at in ats]
        qds = [a_ref[pl.ds(pl.multiple_of(c * 2 * rows, 2 * rows), 2 * rows), :] for c in group]
        boths = [dot(a, kv, 1, 1) for a, kv in zip(qds, kvs)]
        pds = [weigh(b, c) for b, c in zip(boths, group)]
        oqs = [dot(pd, kv) for pd, kv in zip(pds, kvs)]
        backs = [dot(pd, a, 0, 0) for pd, a in zip(pds, qds)]
        for c, oq in zip(group, oqs):
            here = pl.ds(pl.multiple_of(c * rows, rows), rows)
            g_ref[here, 2 * HD :] = jnp.where(first, oq[:rows] * 0.125, oq[rows:]).astype(BF)
        for at, back in zip(ats, backs):
            new = [acc_ref[s, :] + back[j * rows : (j + 1) * rows] for j, s in enumerate(at)]
            for s, v in zip(at, new):
                acc_ref[s, :] = v
        return carry

    lax.fori_loop(0, clusters // GROUP, step, 0)
    g_ref[:, : 2 * HD] = acc_ref[...].astype(BF)

    sum_ref[...] = jnp.zeros_like(sum_ref)

    half = members // 2
    here = lax.broadcasted_iota(jnp.int32, (local, nodes), 0)

    def to_nodes(i, carry):
        picks = [
            (orow_ref[...] == here + owner_ref[i * half + k] * local).astype(F32).astype(BF)
            for k in range(half)
        ]
        back = dot(jnp.concatenate(picks, axis=0), g_ref[...]).astype(BF)
        for k in range(half):
            out_ref[at_owner(i * half + k), :] = back[k * local : (k + 1) * local]
        r = pl.ds(pl.multiple_of(i * half * local, half * local), half * local)
        sum_ref[...] += dot(feat_ref[r, :], back, 0, 0)
        return carry

    lax.fori_loop(0, 2, to_nodes, 0)
    parts, tall, lanes = gw_ref.shape
    deep = tall * 2 // 3
    gw_ref[:, :deep, :] = sum_ref[:, :lanes].reshape(parts, deep, lanes).astype(BF)
    query = sum_ref[:, lanes:].reshape(parts, deep, lanes)
    low, high = query[:, : deep // 2], query[:, deep // 2 :]
    left = lax.broadcasted_iota(jnp.int32, low.shape, 2) < HD
    gw_ref[:, deep:, :] = jnp.where(left, low, pltpu.roll(high, HD, 2)).astype(BF)


def attend(blocks_of, rest, owner, w_head, cot, order, blocks, counts, parts):
    local, width = blocks_of[0].shape[0], blocks_of[0].shape[1] + rest.shape[1]
    nodes = len(blocks_of) * local
    tall, lanes = width // parts * 3 // 2, 2 * HD
    ids = (owner[:, None] * local + jnp.arange(local, dtype=jnp.int32)).reshape(1, nodes)
    vmem = pl.BlockSpec(memory_space=pltpu.VMEM)
    smem = pl.BlockSpec(memory_space=pltpu.SMEM)
    return pl.pallas_call(
        attend_kernel,
        name="attend",
        out_shape=[
            jax.ShapeDtypeStruct((nodes, 4 * HD), BF),
            jax.ShapeDtypeStruct((parts, tall, lanes), BF),
        ],
        in_specs=[smem] * 3 + [vmem] * 5 + [pl.BlockSpec(memory_space=pl.ANY)] * (1 + len(blocks_of)),
        out_specs=[vmem, vmem],
        scratch_shapes=[
            pltpu.VMEM((nodes, width), BF),
            pltpu.VMEM((width, 4 * HD), BF),
            pltpu.VMEM((nodes, 4 * HD), BF),
            pltpu.VMEM((nodes, 2 * HD), BF),
            pltpu.VMEM((2 * nodes, 2 * HD), BF),
            pltpu.VMEM((nodes, 2 * HD), F32),
            pltpu.VMEM((nodes, 4 * HD), BF),
            pltpu.VMEM((width, 4 * HD), F32),
            pltpu.SemaphoreType.DMA((2 * len(blocks_of),)),
        ],
        compiler_params=pltpu.CompilerParams(vmem_limit_bytes=52 << 20),
    )(
        blocks, counts, owner, ids, w_head, cot,
        order.reshape(nodes, 1), order.reshape(1, nodes), rest, *blocks_of,
    )


def finish_kernel(g_ref, w_ref, att_ref, gf_ref, lhs_ref):
    heads = g_ref.shape[0]
    wide = heads * 2 * HD
    first = lax.broadcasted_iota(jnp.int32, (g_ref.shape[1], 2 * HD), 1) < HD
    for h in range(0, heads, 2):
        lhs_ref[:, h * 2 * HD : (h + 1) * 2 * HD] = g_ref[h, :, : 2 * HD]
        lhs_ref[:, (h + 1) * 2 * HD : (h + 2) * 2 * HD] = g_ref[h + 1, :, : 2 * HD]
        even = g_ref[h, :, 2 * HD :].astype(F32)
        odd = g_ref[h + 1, :, 2 * HD :].astype(F32)
        to = slice(h * HD, (h + 2) * HD)
        lhs_ref[:, wide + h * HD : wide + (h + 2) * HD] = jnp.where(
            first, even, pltpu.roll(odd, HD, 1)
        ).astype(BF)
        att_ref[:, to] = jnp.where(first, pltpu.roll(even, HD, 1), odd).astype(BF)
    gf_ref[...] = dot(lhs_ref[...], w_ref[...], 1, 1).astype(BF)


def finish(got, weights):
    rows, width = got.shape[1], weights.shape[0]
    vmem = pl.BlockSpec(memory_space=pltpu.VMEM)
    return pl.pallas_call(
        finish_kernel,
        name="finish",
        out_shape=[
            jax.ShapeDtypeStruct((rows, HEADS * HD), BF),
            jax.ShapeDtypeStruct((rows, width), BF),
        ],
        in_specs=[vmem, vmem],
        out_specs=[vmem, vmem],
        scratch_shapes=[pltpu.VMEM((rows, weights.shape[1]), BF)],
        compiler_params=pltpu.CompilerParams(vmem_limit_bytes=40 << 20),
    )(got, weights)


def reduce_scatter(part, axis, got, weights):
    size = lax.axis_size(axis)
    me = lax.axis_index(axis)
    bit = 1
    while bit < size:
        pairs = part.reshape(-1, 2, *part.shape[1:])
        mine = lax.rem(me // bit, 2)
        keep = lax.dynamic_index_in_dim(pairs, mine, 1, keepdims=False)
        send = lax.dynamic_index_in_dim(pairs, 1 - mine, 1, keepdims=False)
        if 2 * bit == size:
            send, got = lax.optimization_barrier((send, got))
        came = lax.ppermute(send, axis, [(i, i ^ bit) for i in range(size)])
        if 2 * bit == size:
            came, *done = lax.optimization_barrier((came, *finish(got, weights)))
        total = keep.astype(F32) + came.astype(F32)
        part = total.astype(BF)
        bit *= 2
    return total[0], done


def gather_round(block, axis):
    y, x = lax.axis_index(axis) // SIDE, lax.rem(lax.axis_index(axis), SIDE)
    held = {(0, 0): block}
    for (hy, hx), (dy, dx) in HOPS:
        pairs = [
            ((r + dy) % SIDE * SIDE + (c + dx) % SIDE, r * SIDE + c)
            for r in range(SIDE)
            for c in range(SIDE)
        ]
        source = held[hy % SIDE, hx % SIDE]
        held[(hy + dy) % SIDE, (hx + dx) % SIDE] = lax.ppermute(source, axis, pairs)
    places = jnp.asarray(list(held), jnp.int32)
    owner = lax.rem(places[:, 0] + y, SIDE) * SIDE + lax.rem(places[:, 1] + x, SIDE)
    return list(held.values()), owner.astype(jnp.int32)


def per_device(features, qkv_weight, cotangent, node_order, blocks, counts):
    local_rows = features.shape[1]
    model_width = features.shape[2]
    deep = qkv_weight.shape[0]
    feats = features[0]
    head = lax.axis_index("seq")
    by_head = qkv_weight.reshape(deep, HEADS, 3 * HD)
    ordered = jnp.concatenate(
        [by_head[:, :, HD:].reshape(deep, -1), by_head[:, :, :HD].reshape(deep, -1)], axis=1
    )
    size = lax.axis_size("dp")
    core = lax.rem(lax.axis_index("dp"), 2)
    other = lax.ppermute(ordered, "dp", [(i, i ^ 1) for i in range(size)])
    chip = jnp.where(
        core == 0, jnp.stack([ordered, other]), jnp.stack([other, ordered])
    ).reshape(2 * deep, -1)
    groups = [list(range(c, size, 2)) for c in range(2)]
    weights = lax.all_gather(chip, "dp", axis=0, tiled=True, axis_index_groups=groups)
    own = lax.dynamic_slice(chip, (0, head * 2 * HD), (2 * deep, 2 * HD))
    query = lax.dynamic_slice(chip, (0, (2 * HEADS + head) * HD), (2 * deep, HD))
    query = query * jnp.asarray(0.125, BF)
    own = jnp.concatenate(
        [own, jnp.concatenate([query[:deep], query[deep:]], axis=1)], axis=0
    )
    copies = jnp.broadcast_to(own[None], (size // 2, *own.shape))
    w_head = lax.all_to_all(copies, "dp", 0, 0, tiled=True, axis_index_groups=groups)
    half = model_width // 2
    rest = lax.all_gather(feats[:, half:], "seq", axis=0, tiled=True)
    blocks_of, owner = gather_round(feats[:, :half], "seq")
    by_owner = cotangent[0].reshape(local_rows, HEADS, HD).transpose(1, 0, 2)
    by_owner, w_head = lax.optimization_barrier((by_owner, w_head))
    cot = lax.all_to_all(by_owner, "seq", 0, 0, tiled=True).reshape(HEADS * local_rows, HD)
    grads, part = attend(
        blocks_of, rest, owner, w_head, cot, node_order[0], blocks[0], counts[0], size
    )
    got = lax.all_to_all(grads.reshape(HEADS, local_rows, 4 * HD), "seq", 0, 0, tiled=True)
    total, (attended, grad_feats) = reduce_scatter(part, "dp", got, weights)
    query = jnp.concatenate([total[deep:, :HD], total[deep:, HD:]], axis=0)
    grad_weight = jnp.concatenate([query, total[:deep]], axis=1)
    return (
        attended.reshape(1, local_rows, model_width),
        grad_feats.reshape(1, local_rows, model_width),
        grad_weight,
    )


def solution(mesh):
    return jax.shard_map(
        per_device,
        mesh=mesh,
        in_specs=(
            P("dp", "seq", None),
            P("dp", None),
            P("dp", "seq", None),
            P("dp", None),
            P("dp", None, None),
            P("dp", None),
        ),
        out_specs=(P("dp", "seq", None), P("dp", "seq", None), P("dp", "seq")),
        check_vma=False,
    )
```

```python
import jax
import jax.numpy as jnp
from jax import lax
from jax.experimental import pallas as pl
from jax.experimental.pallas import tpu as pltpu
from jax.sharding import PartitionSpec as P

HEADS = 16
HD = 64
BF = jnp.bfloat16
F32 = jnp.float32
ROWS = 1024
GROUP = 24
SIDE = 4
HOPS = (
    ((0, 0), (0, 1)), ((0, 0), (0, -1)), ((0, 0), (1, 0)), ((0, 0), (-1, 0)),
    ((1, 0), (0, 1)), ((-1, 0), (0, -1)), ((0, -1), (1, 0)), ((0, 1), (-1, 0)),
    ((0, 1), (0, 1)), ((1, -1), (0, -1)), ((1, 0), (1, 0)), ((-1, 1), (-1, 0)),
    ((2, 1), (0, 1)), ((-1, -1), (0, -1)), ((1, -1), (1, 0)),
)


def dot(a, b, ca=1, cb=0):
    return lax.dot_general(a, b, (((ca,), (cb,)), ((), ())), preferred_element_type=F32)


def attend_kernel(
    blocks_ref, counts_ref, owner_ref, ids_ref, w_ref, cot_ref, ocol_ref, orow_ref, *refs
):
    members = owner_ref.shape[0]
    parts_refs, refs = refs[:members], refs[members:]
    (out_ref, gw_ref, feat_ref, wide_ref, x_ref, kv_ref, a_ref, acc_ref, g_ref, sum_ref, sem) = refs
    nodes = feat_ref.shape[0]
    clusters, slots = blocks_ref.shape
    rows = nodes // clusters
    keys = slots * rows
    tiles = nodes // ROWS
    local = nodes // members
    loads = [
        pltpu.make_async_copy(part, feat_ref.at[pl.ds(k * local, local), :], sem.at[k])
        for k, part in enumerate(parts_refs)
    ]
    for load in loads:
        load.start()

    chips, tall, lanes = w_ref.shape
    deep = tall * 2 // 3
    wide_ref[:, :lanes] = w_ref[:, :deep, :].reshape(chips * deep, lanes)
    packed = w_ref[:, deep:, :].astype(F32)
    left = lax.broadcasted_iota(jnp.int32, packed.shape, 2) < HD
    query = [jnp.where(left, packed, 0.0), jnp.where(left, pltpu.roll(packed, HD, 2), 0.0)]
    wide_ref[:, lanes:] = jnp.concatenate(query, axis=1).reshape(chips * deep, lanes).astype(BF)
    place = (
        lax.broadcasted_iota(jnp.int32, (HD, 4 * HD), 0) + 3 * HD
        == lax.broadcasted_iota(jnp.int32, (HD, 4 * HD), 1)
    ).astype(F32).astype(BF)

    def at_owner(k):
        return pl.ds(pl.multiple_of(owner_ref[k] * local, local), local)

    batch = 4
    for b in range(0, members, batch):
        for load in loads[b : b + batch]:
            load.wait()
        r = slice(b * local, (b + batch) * local)
        cot = jnp.concatenate([cot_ref[at_owner(b + k), :] for k in range(batch)], axis=0)
        x_ref[r, :] = (dot(feat_ref[r, :], wide_ref[...]) + dot(cot, place)).astype(BF)

    first = lax.broadcasted_iota(jnp.int32, (rows, 2 * HD), 1) < HD

    def to_clusters(i, carry):
        r = pl.ds(pl.multiple_of(i * ROWS, ROWS), ROWS)
        pick = ocol_ref[r, :] == ids_ref[...]
        moved = dot(pick.astype(F32).astype(BF), x_ref[...])
        kv_ref[r, :] = moved[:, : 2 * HD].astype(BF)
        for t in range(ROWS // rows):
            qd = moved[t * rows : (t + 1) * rows, 2 * HD :]
            base = pl.multiple_of(i * 2 * ROWS + 2 * rows * t, 2 * rows)
            a_ref[pl.ds(base, rows), :] = jnp.where(first, qd, 0.0).astype(BF)
            a_ref[pl.ds(base + rows, rows), :] = jnp.where(first, 0.0, qd).astype(BF)
        return carry

    lax.fori_loop(0, tiles, to_clusters, 0)

    acc_ref[...] = jnp.zeros_like(acc_ref)
    place_of = lax.broadcasted_iota(jnp.int32, (rows, keys), 1)

    def weigh(both, c):
        score = jnp.where(place_of < counts_ref[c] * rows, both[:rows], -1e30)
        dpw = both[rows:]
        raw = jnp.exp(score - jnp.max(score, axis=1, keepdims=True))
        p = raw * (1.0 / jnp.sum(raw, axis=1, keepdims=True))
        ds = p * (dpw - jnp.sum(p * dpw, axis=1, keepdims=True))
        return jnp.concatenate([ds, p], axis=0).astype(BF)

    def step(i, carry):
        group = [i * GROUP + u for u in range(GROUP)]
        ats = [
            [pl.ds(pl.multiple_of(blocks_ref[c, j] * rows, rows), rows) for j in range(slots)]
            for c in group
        ]
        kvs = [jnp.concatenate([kv_ref[s, :] for s in at], axis=0) for at in ats]
        qds = [a_ref[pl.ds(pl.multiple_of(c * 2 * rows, 2 * rows), 2 * rows), :] for c in group]
        boths = [dot(a, kv, 1, 1) for a, kv in zip(qds, kvs)]
        pds = [weigh(b, c) for b, c in zip(boths, group)]
        oqs = [dot(pd, kv) for pd, kv in zip(pds, kvs)]
        backs = [dot(pd, a, 0, 0) for pd, a in zip(pds, qds)]
        for c, oq in zip(group, oqs):
            here = pl.ds(pl.multiple_of(c * rows, rows), rows)
            g_ref[here, 2 * HD :] = jnp.where(first, oq[:rows] * 0.125, oq[rows:]).astype(BF)
        for at, back in zip(ats, backs):
            new = [acc_ref[s, :] + back[j * rows : (j + 1) * rows] for j, s in enumerate(at)]
            for s, v in zip(at, new):
                acc_ref[s, :] = v
        return carry

    lax.fori_loop(0, clusters // GROUP, step, 0)
    g_ref[:, : 2 * HD] = acc_ref[...].astype(BF)

    sum_ref[...] = jnp.zeros_like(sum_ref)

    half = members // 2
    here = lax.broadcasted_iota(jnp.int32, (local, nodes), 0)

    def to_nodes(i, carry):
        picks = [
            (orow_ref[...] == here + owner_ref[i * half + k] * local).astype(F32).astype(BF)
            for k in range(half)
        ]
        back = dot(jnp.concatenate(picks, axis=0), g_ref[...]).astype(BF)
        for k in range(half):
            out_ref[at_owner(i * half + k), :] = back[k * local : (k + 1) * local]
        r = pl.ds(pl.multiple_of(i * half * local, half * local), half * local)
        sum_ref[...] += dot(feat_ref[r, :], back, 0, 0)
        return carry

    lax.fori_loop(0, 2, to_nodes, 0)
    parts, tall, lanes = gw_ref.shape
    deep = tall * 2 // 3
    gw_ref[:, :deep, :] = sum_ref[:, :lanes].reshape(parts, deep, lanes).astype(BF)
    query = sum_ref[:, lanes:].reshape(parts, deep, lanes)
    low, high = query[:, : deep // 2], query[:, deep // 2 :]
    left = lax.broadcasted_iota(jnp.int32, low.shape, 2) < HD
    gw_ref[:, deep:, :] = jnp.where(left, low, pltpu.roll(high, HD, 2)).astype(BF)


def attend(blocks_of, owner, w_head, cot, order, blocks, counts, parts):
    local, width = blocks_of[0].shape
    nodes = len(blocks_of) * local
    tall, lanes = width // parts * 3 // 2, 2 * HD
    ids = (owner[:, None] * local + jnp.arange(local, dtype=jnp.int32)).reshape(1, nodes)
    vmem = pl.BlockSpec(memory_space=pltpu.VMEM)
    smem = pl.BlockSpec(memory_space=pltpu.SMEM)
    return pl.pallas_call(
        attend_kernel,
        name="attend",
        out_shape=[
            jax.ShapeDtypeStruct((nodes, 4 * HD), BF),
            jax.ShapeDtypeStruct((parts, tall, lanes), BF),
        ],
        in_specs=[smem] * 3 + [vmem] * 5 + [pl.BlockSpec(memory_space=pl.ANY)] * len(blocks_of),
        out_specs=[vmem, vmem],
        scratch_shapes=[
            pltpu.VMEM((nodes, width), BF),
            pltpu.VMEM((width, 4 * HD), BF),
            pltpu.VMEM((nodes, 4 * HD), BF),
            pltpu.VMEM((nodes, 2 * HD), BF),
            pltpu.VMEM((2 * nodes, 2 * HD), BF),
            pltpu.VMEM((nodes, 2 * HD), F32),
            pltpu.VMEM((nodes, 4 * HD), BF),
            pltpu.VMEM((width, 4 * HD), F32),
            pltpu.SemaphoreType.DMA((len(blocks_of),)),
        ],
        compiler_params=pltpu.CompilerParams(vmem_limit_bytes=52 << 20),
    )(
        blocks, counts, owner, ids, w_head, cot,
        order.reshape(nodes, 1), order.reshape(1, nodes), *blocks_of,
    )


def finish_kernel(g_ref, w_ref, att_ref, gf_ref, lhs_ref, have_ref, sem):
    bands = sem.shape[0]
    band = w_ref.shape[0] // bands
    cuts = [slice(i * band, (i + 1) * band) for i in range(bands)]
    loads = [
        pltpu.make_async_copy(w_ref.at[cut, :], have_ref.at[cut, :], sem.at[i])
        for i, cut in enumerate(cuts)
    ]
    for load in loads:
        load.start()
    heads = g_ref.shape[0]
    wide = heads * 2 * HD
    first = lax.broadcasted_iota(jnp.int32, (g_ref.shape[1], 2 * HD), 1) < HD
    for h in range(0, heads, 2):
        lhs_ref[:, h * 2 * HD : (h + 1) * 2 * HD] = g_ref[h, :, : 2 * HD]
        lhs_ref[:, (h + 1) * 2 * HD : (h + 2) * 2 * HD] = g_ref[h + 1, :, : 2 * HD]
        even = g_ref[h, :, 2 * HD :].astype(F32)
        odd = g_ref[h + 1, :, 2 * HD :].astype(F32)
        to = slice(h * HD, (h + 2) * HD)
        lhs_ref[:, wide + h * HD : wide + (h + 2) * HD] = jnp.where(
            first, even, pltpu.roll(odd, HD, 1)
        ).astype(BF)
        att_ref[:, to] = jnp.where(first, pltpu.roll(even, HD, 1), odd).astype(BF)
    for cut, load in zip(cuts, loads):
        load.wait()
        gf_ref[:, cut] = dot(lhs_ref[...], have_ref[cut, :], 1, 1).astype(BF)


def finish(got, weights):
    rows, width = got.shape[1], weights.shape[0]
    vmem = pl.BlockSpec(memory_space=pltpu.VMEM)
    return pl.pallas_call(
        finish_kernel,
        name="finish",
        out_shape=[
            jax.ShapeDtypeStruct((rows, HEADS * HD), BF),
            jax.ShapeDtypeStruct((rows, width), BF),
        ],
        in_specs=[vmem, pl.BlockSpec(memory_space=pl.ANY)],
        out_specs=[vmem, vmem],
        scratch_shapes=[
            pltpu.VMEM((rows, weights.shape[1]), BF),
            pltpu.VMEM(weights.shape, BF),
            pltpu.SemaphoreType.DMA((4,)),
        ],
        compiler_params=pltpu.CompilerParams(vmem_limit_bytes=57 << 20),
    )(got, weights)


def reduce_scatter(part, axis, got, weights):
    size = lax.axis_size(axis)
    me = lax.axis_index(axis)
    bit = 1
    while bit < size:
        pairs = part.reshape(-1, 2, *part.shape[1:])
        mine = lax.rem(me // bit, 2)
        keep = lax.dynamic_index_in_dim(pairs, mine, 1, keepdims=False)
        send = lax.dynamic_index_in_dim(pairs, 1 - mine, 1, keepdims=False)
        if 2 * bit == size:
            send, got = lax.optimization_barrier((send, got))
        came = lax.ppermute(send, axis, [(i, i ^ bit) for i in range(size)])
        if 2 * bit == size:
            came, *done = lax.optimization_barrier((came, *finish(got, weights)))
        total = keep.astype(F32) + came.astype(F32)
        part = total.astype(BF)
        bit *= 2
    return total[0], done


def gather_round(block, axis):
    y, x = lax.axis_index(axis) // SIDE, lax.rem(lax.axis_index(axis), SIDE)
    held = {(0, 0): block}
    for (hy, hx), (dy, dx) in HOPS:
        pairs = [
            ((r + dy) % SIDE * SIDE + (c + dx) % SIDE, r * SIDE + c)
            for r in range(SIDE)
            for c in range(SIDE)
        ]
        source = held[hy % SIDE, hx % SIDE]
        held[(hy + dy) % SIDE, (hx + dx) % SIDE] = lax.ppermute(source, axis, pairs)
    places = jnp.asarray(list(held), jnp.int32)
    owner = lax.rem(places[:, 0] + y, SIDE) * SIDE + lax.rem(places[:, 1] + x, SIDE)
    return list(held.values()), owner.astype(jnp.int32)


def per_device(features, qkv_weight, cotangent, node_order, blocks, counts):
    local_rows = features.shape[1]
    model_width = features.shape[2]
    deep = qkv_weight.shape[0]
    feats = features[0]
    head = lax.axis_index("seq")
    by_head = qkv_weight.reshape(deep, HEADS, 3 * HD)
    ordered = jnp.concatenate(
        [by_head[:, :, HD:].reshape(deep, -1), by_head[:, :, :HD].reshape(deep, -1)], axis=1
    )
    size = lax.axis_size("dp")
    core = lax.rem(lax.axis_index("dp"), 2)
    other = lax.ppermute(ordered, "dp", [(i, i ^ 1) for i in range(size)])
    chip = jnp.where(
        core == 0, jnp.stack([ordered, other]), jnp.stack([other, ordered])
    ).reshape(2 * deep, -1)
    groups = [list(range(c, size, 2)) for c in range(2)]
    weights = lax.all_gather(chip, "dp", axis=0, tiled=True, axis_index_groups=groups)
    own = lax.dynamic_slice(chip, (0, head * 2 * HD), (2 * deep, 2 * HD))
    query = lax.dynamic_slice(chip, (0, (2 * HEADS + head) * HD), (2 * deep, HD))
    query = query * jnp.asarray(0.125, BF)
    own = jnp.concatenate(
        [own, jnp.concatenate([query[:deep], query[deep:]], axis=1)], axis=0
    )
    copies = jnp.broadcast_to(own[None], (size // 2, *own.shape))
    w_head = lax.all_to_all(copies, "dp", 0, 0, tiled=True, axis_index_groups=groups)
    blocks_of, owner = gather_round(feats, "seq")
    by_owner = cotangent[0].reshape(local_rows, HEADS, HD).transpose(1, 0, 2)
    by_owner, w_head = lax.optimization_barrier((by_owner, w_head))
    cot = lax.all_to_all(by_owner, "seq", 0, 0, tiled=True).reshape(HEADS * local_rows, HD)
    grads, part = attend(
        blocks_of, owner, w_head, cot, node_order[0], blocks[0], counts[0], size
    )
    got = lax.all_to_all(grads.reshape(HEADS, local_rows, 4 * HD), "seq", 0, 0, tiled=True)
    total, (attended, grad_feats) = reduce_scatter(part, "dp", got, weights)
    query = jnp.concatenate([total[deep:, :HD], total[deep:, HD:]], axis=0)
    grad_weight = jnp.concatenate([query, total[:deep]], axis=1)
    return (
        attended.reshape(1, local_rows, model_width),
        grad_feats.reshape(1, local_rows, model_width),
        grad_weight,
    )


def solution(mesh):
    return jax.shard_map(
        per_device,
        mesh=mesh,
        in_specs=(
            P("dp", "seq", None),
            P("dp", None),
            P("dp", "seq", None),
            P("dp", None),
            P("dp", None, None),
            P("dp", None),
        ),
        out_specs=(P("dp", "seq", None), P("dp", "seq", None), P("dp", "seq")),
        check_vma=False,
    )
```
